512 devices in a mesh: seq: 32 (over y, x), head: 16 (over z, core).
Axes of the slice: x: 4, y: 8, z: 8, core: 2. Of those that a mesh axis runs over, the one named last changes fastest.
Arguments:
- queries: bfloat16 [8192, 8192], P('seq', 'head'), may hold values from -1.796875 to 1.796875
- key_rows: bfloat16 [8192, 8192], P('seq', 'head'), may hold values from -1.796875 to 1.796875
- value_rows: bfloat16 [8192, 8192], P('seq', 'head'), may hold values from -6 to 6
- level_table: float32 [64, 7, 64], P(None, None, 'head'), may hold values from 0.25 to 4
- level_index: int32 [8192, 7], P('seq'), may hold values from 0 to 63
- norm_gain: float32 [8192], replicated, may hold values from 0.5 to 1.5
- cotangent: bfloat16 [8192, 8192], P(('seq', 'head')), may hold values from -6 to 6
Outputs:
- normed: bfloat16 [8192, 8192], P(('seq', 'head'))
- grad_query: bfloat16 [8192, 8192], P('seq', 'head')
- grad_key: bfloat16 [8192, 8192], P('seq', 'head')
- grad_value: bfloat16 [8192, 8192], P('seq', 'head')
- grad_table: float32 [64, 7, 64], P(None, None, 'head')
- grad_gain: float32 [8192], replicated
The draws below stay inside these ranges and needn't reach their ends.
All inputs are finite; a program needn't handle non-finite values.
Results may differ from the reference program's by a relative error of at most 0.014.
Values may be sent and summed in bfloat16 or wider, within the bound.
No kernel may reach another device: no remote copies, remote signals or barrier semaphores. Data moves between devices by JAX's collectives and lax.ppermute only.
A program may use at most 64 MiB of HBM per device.

```python
import math
import jax
import jax.numpy as jnp
from jax import lax

HEADS = 64
DH = 128
CH = 128
LEVELS = 7
TABLE = 64
TOKENS = 8192


def set_ends(entries, stream_key, low, largest):
    longest = entries.shape.index(max(entries.shape))
    spots = []
    for shift in (0, 1):
        where = [jax.random.randint(jax.random.fold_in(stream_key, axis), (), 0, length) for axis, length in enumerate(entries.shape)]
        where[longest] = (where[longest] + shift) % entries.shape[longest]
        spots.append(tuple(where))
    return entries.at[spots[0]].set(low).at[spots[1]].set(largest)


def shard_levels(rng, extent, pieces, least, largest):
    def one(dim, parts):
        steps = jax.random.uniform(jax.random.fold_in(jax.random.fold_in(rng, 6), dim), (parts,), jnp.float32, least / len(pieces), largest / len(pieces))
        return jnp.repeat(jnp.exp(steps), extent[dim] // parts).reshape((-1,) + (1,) * (len(extent) - dim - 1))

    factor_of = one(*pieces[0])
    for cut in pieces[1:]:
        factor_of = factor_of * one(*cut)
    return factor_of


def gaussian(stream_key, extent, deviation, most, split=(), kind=jnp.bfloat16):
    array = jax.random.normal(stream_key, extent, jnp.float32) * deviation
    if len(split) > 0:
        array = shard_levels(stream_key, extent, split, -0.22, 0.18) * array
    return jnp.clip(array, min=-most, max=most).astype(kind)


def setup_inputs(seed: int = 0) -> dict:
    splits = jax.random.split(jax.random.key(seed), 8)
    queries = gaussian(splits[0], (TOKENS, HEADS * DH), 0.3, 1.796875, ((0, 32), (1, 16)))
    key_rows = gaussian(splits[1], (TOKENS, HEADS * DH), 0.3, 1.796875, ((0, 32), (1, 16)))
    value_rows = gaussian(splits[2], (TOKENS, HEADS * DH), 1.0, 6.0, ((0, 32), (1, 16)))
    level_table = jnp.clip(jnp.exp(math.log(4.0) - 2.7725887 * jax.random.uniform(splits[3], (TABLE, LEVELS, HEADS), jnp.float32) ** shard_levels(splits[3], (TABLE, LEVELS, HEADS), ((2, 16),), -0.2, 0.2)), 0.25, 4.0)
    level_index = set_ends(jax.random.randint(splits[4], (TOKENS, LEVELS), 0, TABLE), jax.random.fold_in(splits[4], 1), 0, TABLE - 1).astype(jnp.int32)
    norm_gain = jnp.clip(1.0 + 0.1 * jax.random.normal(splits[5], (HEADS * DH,), jnp.float32), 0.5, 1.5)
    cotangent = gaussian(splits[6], (TOKENS, HEADS * DH), 1.0, 6.0, ((0, 512),))
    return {"queries": queries, "key_rows": key_rows, "value_rows": value_rows, "level_table": level_table, "level_index": level_index, "norm_gain": norm_gain, "cotangent": cotangent}


EPSILON = 1e-06
HIGHEST = lax.Precision.HIGHEST

def rounded(values):
    return lax.optimization_barrier(values.astype(jnp.bfloat16)).astype(jnp.float32)

def causal_mask():
    row_ids = lax.broadcasted_iota(jnp.int32, (CH, CH), 0)
    col_ids = lax.broadcasted_iota(jnp.int32, (CH, CH), 1)
    return col_ids <= row_ids

def query_side(span_states):
    span_count = span_states.shape[0]
    zeros_row = jnp.zeros((1,) + span_states.shape[1:], jnp.float32)
    prefix = jnp.concatenate([zeros_row, jnp.cumsum(span_states, axis=0)], axis=0)
    span_ids = jnp.arange(span_count, dtype=jnp.int32)
    layers = []
    for level_no in range(1, LEVELS):
        if level_no < LEVELS - 1:
            block_start = jnp.left_shift(jnp.right_shift(span_ids, level_no), level_no)
            middle = jnp.minimum(block_start + (1 << level_no - 1), span_count).astype(jnp.int32)
            active = jnp.bitwise_and(jnp.right_shift(span_ids, level_no - 1), 1).astype(jnp.float32)
            layers.append((prefix[middle] - prefix[block_start]) * active[:, None, None])
        else:
            block_start = jnp.left_shift(jnp.right_shift(span_ids, level_no - 1), level_no - 1)
            layers.append(prefix[block_start])
    return jnp.stack(layers, axis=1)

def key_side(query_grads):
    span_count = query_grads.shape[0]
    span_ids = jnp.arange(span_count, dtype=jnp.int32)
    result = jnp.zeros(query_grads.shape[:1] + query_grads.shape[2:], jnp.float32)
    for level_no in range(1, LEVELS):
        part = query_grads[:, level_no - 1]
        zeros_row = jnp.zeros((1,) + part.shape[1:], jnp.float32)
        prefix = jnp.concatenate([zeros_row, jnp.cumsum(part, axis=0)], axis=0)
        if level_no < LEVELS - 1:
            aligned = jnp.left_shift(jnp.right_shift(span_ids, level_no), level_no)
            block_start = jnp.minimum(aligned + (1 << level_no - 1), span_count).astype(jnp.int32)
            block_stop = jnp.minimum(aligned + (1 << level_no), span_count).astype(jnp.int32)
            active = 1.0 - jnp.bitwise_and(jnp.right_shift(span_ids, level_no - 1), 1).astype(jnp.float32)
            result = result + (prefix[block_stop] - prefix[block_start]) * active[:, None, None]
        else:
            block_start = jnp.left_shift(jnp.right_shift(span_ids, level_no - 1) + 1, level_no - 1)
            block_start = jnp.minimum(block_start, span_count).astype(jnp.int32)
            result = result + (prefix[span_count] - prefix[block_start])
    return result

def head_forward(query_head, key_head, value_head, weight_head):
    query_f = query_head.astype(jnp.float32)
    key_f = key_head.astype(jnp.float32)
    value_f = value_head.astype(jnp.float32)
    span_states = jnp.einsum('ica,icb->iab', key_f, value_f, precision=HIGHEST)
    states = rounded(query_side(span_states))
    far_out = jnp.einsum('ica,ilab->iclb', query_f, states, precision=HIGHEST)
    scores = jnp.einsum('ica,ina->icn', query_f, key_f, precision=HIGHEST)
    scores = jnp.where(causal_mask()[None], scores, 0.0)
    near_out = jnp.einsum('icn,inb->icb', rounded(scores), value_f, precision=HIGHEST)
    level_out = jnp.concatenate([near_out[:, :, None], far_out], axis=2)
    attn = lax.optimization_barrier(jnp.sum(weight_head[..., None] * level_out, axis=2))
    return (attn.astype(jnp.bfloat16), level_out, states, scores)

def head_backward(query_head, key_head, value_head, weight_head, grad_head):
    attn, level_out, states, scores = head_forward(query_head, key_head, value_head, weight_head)
    query_f = query_head.astype(jnp.float32)
    key_f = key_head.astype(jnp.float32)
    value_f = value_head.astype(jnp.float32)
    grad_f = grad_head.astype(jnp.float32)
    causal = causal_mask()[None]
    grad_weight = lax.optimization_barrier(jnp.sum(level_out * grad_f[:, :, None], axis=3))
    along_values = jnp.einsum('icb,inb->icn', grad_f, value_f, precision=HIGHEST)
    first_weight = weight_head[:, :, 0][:, :, None]
    grad_scores = rounded(jnp.where(causal, along_values * first_weight, 0.0))
    weighted_scores = rounded(jnp.where(causal, scores * first_weight, 0.0))
    near_dq = jnp.einsum('icn,ina->ica', grad_scores, key_f, precision=HIGHEST)
    near_dk = jnp.einsum('icn,ica->ina', grad_scores, query_f, precision=HIGHEST)
    near_dv = jnp.einsum('icn,icb->inb', weighted_scores, grad_f, precision=HIGHEST)
    far_dq = jnp.einsum('icb,ilab->icla', grad_f, states, precision=HIGHEST)
    grad_query = (near_dq + lax.optimization_barrier(jnp.sum(weight_head[:, :, 1:, None] * far_dq, axis=2))).astype(jnp.bfloat16)
    scaled_grad = rounded(weight_head[:, :, 1:, None] * grad_f[:, :, None])
    query_grads = jnp.einsum('ica,iclb->ilab', query_f, scaled_grad, precision=HIGHEST)
    key_state = rounded(key_side(query_grads))
    grad_key = (near_dk + jnp.einsum('jab,jnb->jna', key_state, value_f, precision=HIGHEST)).astype(jnp.bfloat16)
    grad_value = (near_dv + jnp.einsum('jab,jna->jnb', key_state, key_f, precision=HIGHEST)).astype(jnp.bfloat16)
    return (grad_query, grad_key, grad_value, grad_weight)

def split_heads(rows):
    return rows.reshape(TOKENS, HEADS, DH).transpose(1, 0, 2).reshape(HEADS, TOKENS // CH, CH, DH)

def join_heads(blocks):
    return blocks.reshape(HEADS, TOKENS, DH).transpose(1, 0, 2).reshape(TOKENS, HEADS * DH)

def reference(queries, key_rows, value_rows, level_table, level_index, norm_gain, cotangent):
    onehot = (level_index[:, :, None] == jnp.arange(TABLE, dtype=jnp.int32)[None, None, :]).astype(jnp.float32)
    weights = jnp.einsum('tlx,xlh->htl', onehot, level_table.astype(jnp.float32), precision=HIGHEST)
    weights = weights.reshape(HEADS, TOKENS // CH, CH, LEVELS)
    query_heads = split_heads(queries)
    key_heads = split_heads(key_rows)
    value_heads = split_heads(value_rows)

    def forward_one(operands):
        return head_forward(operands[0], operands[1], operands[2], operands[3])[0]
    attn = join_heads(lax.map(forward_one, (query_heads, key_heads, value_heads, weights)))
    attn_f = attn.astype(jnp.float32)
    inv_rms = lax.rsqrt(lax.optimization_barrier(jnp.mean(attn_f * attn_f, axis=1, keepdims=True)) + EPSILON)
    unit_rows = attn_f * inv_rms
    gain_f = norm_gain.astype(jnp.float32)
    normed = (unit_rows * gain_f).astype(jnp.bfloat16)
    grad_out = cotangent.astype(jnp.float32)
    scaled = grad_out * gain_f
    grad_gain = lax.optimization_barrier(jnp.sum(grad_out * unit_rows, axis=0))
    grad_attn = ((scaled - unit_rows * lax.optimization_barrier(jnp.mean(scaled * unit_rows, axis=1, keepdims=True))) * inv_rms).astype(jnp.bfloat16)
    grad_heads = split_heads(grad_attn)

    def backward_one(operands):
        return head_backward(operands[0], operands[1], operands[2], operands[3], operands[4])
    grad_query, grad_key, grad_value, grad_weight = lax.map(backward_one, (query_heads, key_heads, value_heads, weights, grad_heads))
    grad_table = jnp.einsum('tlx,htl->xlh', onehot, grad_weight.reshape(HEADS, TOKENS, LEVELS), precision=HIGHEST)
    return (normed, join_heads(grad_query), join_heads(grad_key), join_heads(grad_value), grad_table, grad_gain)
```

```python
import jax
import jax.numpy as jnp
from jax import lax
from jax.experimental import pallas as pl
from jax.experimental.pallas import tpu as pltpu
from jax.sharding import PartitionSpec as P

CH = 128
TABLE = 64
EPSILON = 1e-06
HIGHEST = lax.Precision.HIGHEST
F32 = jnp.float32
BF16 = jnp.bfloat16
INTERPRET = False


def call(kernel, name, out_shape, *operands):
    return pl.pallas_call(
        kernel,
        out_shape=out_shape,
        name=name,
        interpret=INTERPRET,
        compiler_params=pltpu.CompilerParams(vmem_limit_bytes=48 * 1024 * 1024),
    )(*operands)


def shaped(shape, dtype):
    return jax.ShapeDtypeStruct(shape, dtype)


def dot_nn(a, b, precision=None):
    return lax.dot_general(a, b, (((1,), (0,)), ((), ())), precision=precision, preferred_element_type=F32)


def dot_nt(a, b):
    return lax.dot_general(a, b, (((1,), (1,)), ((), ())), preferred_element_type=F32)


def dot_tn(a, b, precision=None):
    return lax.dot_general(a, b, (((0,), (0,)), ((), ())), precision=precision, preferred_element_type=F32)


def causal_mask():
    rows = lax.broadcasted_iota(jnp.int32, (CH, CH), 0)
    cols = lax.broadcasted_iota(jnp.int32, (CH, CH), 1)
    return cols <= rows


def span_rows(c):
    return slice(c * CH, (c + 1) * CH)


def to_row(tile):
    return jnp.sum(tile.T, axis=0, keepdims=True)


def to_columns(row):
    return jnp.broadcast_to(row, (CH, CH)).T


def put_slices(ref, value, head, level=None):
    slices, height = ref.shape[0], ref.shape[-2]
    per_head = CH // height
    pieces = value.astype(BF16).reshape(per_head, height, value.shape[1])
    where = slice(head * per_head, (head + 1) * per_head)
    if level is None:
        ref[where] = pieces
    else:
        ref[where, level] = pieces


def get_slices(ref, head, level=None):
    height, width = ref.shape[-2:]
    per_head = CH // height
    where = slice(head * per_head, (head + 1) * per_head)
    pieces = ref[where] if level is None else ref[where, level]
    return pieces.reshape(CH, width)


def state_kernel(key_ref, value_ref, total_ref, first_ref):
    heads = key_ref.shape[1] // CH
    for h in range(heads):
        cols = span_rows(h)
        first = dot_tn(key_ref[0:CH, cols], value_ref[0:CH, cols])
        second = dot_tn(key_ref[CH : 2 * CH, cols], value_ref[CH : 2 * CH, cols])
        first_ref[cols, :] = first.astype(BF16)
        put_slices(total_ref, first + second, h)


def prefix_kernel(in_ref, out_ref):
    shards, levels = out_ref.shape[0], out_ref.shape[1]
    sums = [in_ref[s].astype(F32) for s in range(shards)]
    zero = jnp.zeros(in_ref.shape[1:], BF16)
    for level in range(levels):
        rounded = [s.astype(BF16) for s in sums]
        for t in range(shards):
            group = t >> level
            out_ref[t, level] = rounded[group - 1] if group & 1 else zero
        sums = [sums[2 * i] + sums[2 * i + 1] for i in range(len(sums) // 2)]


def suffix_kernel(in_ref, out_ref):
    shards, levels = in_ref.shape[0], in_ref.shape[1]
    carried = [None]
    for level in range(levels - 1, -1, -1):
        size = 1 << level
        groups = shards >> level
        below = []
        for g in range(groups):
            base = carried[g >> 1]
            if g & 1 == 0:
                total = None
                for s in range((g + 1) * size, (g + 2) * size):
                    piece = in_ref[s, level].astype(F32)
                    total = piece if total is None else total + piece
                base = total if base is None else base + total
            below.append(base)
        carried = below
    zero = jnp.zeros(in_ref.shape[2:], F32)
    for t in range(shards):
        value = zero if carried[t] is None else carried[t]
        out_ref[t] = value.astype(BF16)


def weight_kernel(index_ref, table_ref, weight_ref):
    levels = index_ref.shape[1]
    heads = table_ref.shape[1]
    tokens = index_ref.shape[0]
    entry = lax.broadcasted_iota(jnp.int32, (tokens, TABLE), 1)
    for level in range(levels):
        onehot = (index_ref[:, level : level + 1] == entry).astype(F32)
        picked = dot_nn(onehot, table_ref[level * TABLE : (level + 1) * TABLE, :], HIGHEST)
        weight_ref[:, level * heads : (level + 1) * heads] = picked


def near_kernel(query_ref, key_ref, value_ref, first_ref, weight_ref, out_ref):
    heads = query_ref.shape[1] // CH
    spans = query_ref.shape[0] // CH
    causal = causal_mask()
    for c in range(spans):
        rows = span_rows(c)
        for h in range(heads):
            cols = span_rows(h)
            query = query_ref[rows, cols]
            scores = jnp.where(causal, dot_nt(query, key_ref[rows, cols]), 0.0).astype(BF16)
            near = weight_ref[rows, h : h + 1] * dot_nn(scores, value_ref[rows, cols])
            if c == 1:
                near = near + weight_ref[rows, heads + h : heads + h + 1] * dot_nn(query, first_ref[cols, :])
            out_ref[rows, cols] = near


def far_kernel(near_ref, query_ref, state_ref, weight_ref, cot_ref, gain_ref, attn_ref, stat_ref):
    heads = query_ref.shape[1] // CH
    spans = query_ref.shape[0] // CH
    levels = state_ref.shape[1]
    stats = []
    for c in range(spans):
        rows = span_rows(c)
        squares = jnp.zeros((CH, CH), F32)
        along = jnp.zeros((CH, CH), F32)
        for h in range(heads):
            cols = span_rows(h)
            query = query_ref[rows, cols]
            total = near_ref[rows, cols]
            for level in range(levels):
                spot = (level + 2) * heads + h
                total = total + weight_ref[rows, spot : spot + 1] * dot_nn(query, get_slices(state_ref, h, level))
            attn = total.astype(BF16)
            attn_ref[rows, cols] = attn
            attn_f = attn.astype(F32)
            scaled = cot_ref[rows, cols].astype(F32) * gain_ref[:, cols]
            squares = squares + attn_f * attn_f
            along = along + scaled * attn_f
        stats.append(to_row(squares))
        stats.append(to_row(along))
    block = jnp.concatenate(stats + [jnp.zeros((8 - len(stats), CH), F32)], axis=0)
    for d in range(stat_ref.shape[0]):
        stat_ref[d] = block


def norm_columns(stat_ref, features, c):
    total = stat_ref[0]
    for d in range(1, stat_ref.shape[0]):
        total = total + stat_ref[d]
    inv_rms = lax.rsqrt(total[2 * c : 2 * c + 1, :] / features + EPSILON)
    mean = total[2 * c + 1 : 2 * c + 2, :] * inv_rms / features
    return to_columns(inv_rms), to_columns(mean)


def grad_kernel(attn_ref, stat_ref, cot_ref, gain_ref, query_ref, weight_ref, grad_ref, group_ref):
    heads = query_ref.shape[1] // CH
    spans = query_ref.shape[0] // CH
    levels = group_ref.shape[1]
    features = float(stat_ref.shape[0] * attn_ref.shape[1])
    norms = [norm_columns(stat_ref, features, c) for c in range(spans)]
    for h in range(heads):
        cols = span_rows(h)
        parts = [[] for _ in range(levels)]
        for c in range(spans):
            rows = span_rows(c)
            inv_rms, mean = norms[c]
            unit = attn_ref[rows, cols].astype(F32) * inv_rms
            scaled = cot_ref[rows, cols].astype(F32) * gain_ref[:, cols]
            grad = ((scaled - unit * mean) * inv_rms).astype(BF16)
            grad_ref[rows, cols] = grad
            grad_f = grad.astype(F32)
            for level in range(levels):
                spot = (level + 2) * heads + h
                parts[level].append((weight_ref[rows, spot : spot + 1] * grad_f).astype(BF16))
        query = query_ref[:, cols]
        for level in range(levels):
            put_slices(group_ref, dot_tn(query, jnp.concatenate(parts[level], axis=0)), h, level)


def norm_kernel(attn_ref, stat_ref, cot_ref, gain_ref, normed_ref, gain_part_ref):
    heads = attn_ref.shape[1] // CH
    spans = attn_ref.shape[0] // CH
    features = float(stat_ref.shape[0] * attn_ref.shape[1])
    norms = [norm_columns(stat_ref, features, c) for c in range(spans)]
    pieces = []
    for h in range(heads):
        cols = span_rows(h)
        part = jnp.zeros((1, CH), F32)
        for c in range(spans):
            rows = span_rows(c)
            unit = attn_ref[rows, cols].astype(F32) * norms[c][0]
            normed_ref[rows, cols] = (unit * gain_ref[:, cols]).astype(BF16)
            part = part + jnp.sum(cot_ref[rows, cols].astype(F32) * unit, axis=0, keepdims=True)
        pieces.append(part)
    block = jnp.concatenate(pieces + [jnp.zeros((8 - heads, CH), F32)], axis=0)
    for d in range(gain_part_ref.shape[0]):
        gain_part_ref[d] = block


def back_kernel(
    query_ref, key_ref, value_ref, grad_ref, weight_ref, state_ref, first_ref, index_ref,
    dq_ref, dk_ref, dv_ref, inner_ref, table_ref, gw_ref,
):
    heads = query_ref.shape[1] // CH
    spans = query_ref.shape[0] // CH
    levels = state_ref.shape[1]
    all_levels = levels + 2
    tokens = spans * CH
    causal = causal_mask()
    gw_ref[...] = jnp.zeros(gw_ref.shape, F32)
    for c in range(spans):
        rows = span_rows(c)
        for h in range(heads):
            cols = span_rows(h)
            query = query_ref[rows, cols]
            query_f = query.astype(F32)
            key = key_ref[rows, cols]
            grad = grad_ref[rows, cols]
            first_weight = weight_ref[rows, h : h + 1]
            scores = jnp.where(causal, dot_nt(query, key), 0.0)
            along = jnp.where(causal, dot_nt(grad, value_ref[rows, cols]), 0.0)
            gw_ref[rows, h : h + 1] = jnp.sum(scores.astype(BF16).astype(F32) * along, axis=1, keepdims=True)
            grad_scores = (along * first_weight).astype(BF16)
            weighted = (scores * first_weight).astype(BF16)
            dq = dot_nn(grad_scores, key)
            dk_ref[rows, cols] = dot_tn(grad_scores, query)
            dv_ref[rows, cols] = dot_tn(weighted, grad)
            if c == 1:
                spot = heads + h
                weight = weight_ref[rows, spot : spot + 1]
                far = dot_nt(grad, first_ref[cols, :])
                gw_ref[rows, spot : spot + 1] = jnp.sum(query_f * far, axis=1, keepdims=True)
                dq = dq + weight * far
                inner_ref[cols, :] = dot_tn(query, (weight * grad.astype(F32)).astype(BF16))
            for level in range(levels):
                spot = (level + 2) * heads + h
                far = dot_nt(grad, get_slices(state_ref, h, level))
                gw_ref[rows, spot : spot + 1] = jnp.sum(query_f * far, axis=1, keepdims=True)
                dq = dq + weight_ref[rows, spot : spot + 1] * far
            dq_ref[rows, cols] = dq.astype(BF16)
    grads = gw_ref[...]
    entry = lax.broadcasted_iota(jnp.int32, (tokens, TABLE), 1)
    width = grads.shape[1]
    pick_rows = lax.broadcasted_iota(jnp.int32, (8, width), 0)
    pick_cols = lax.broadcasted_iota(jnp.int32, (8, width), 1)
    blocks = []
    for level in range(all_levels):
        onehot = (index_ref[:, level : level + 1] == entry).astype(F32)
        by_row = dot_tn(grads, onehot, HIGHEST)
        pick = ((pick_cols == pick_rows + level * heads) & (pick_rows < heads)).astype(F32)
        blocks.append(dot_nn(pick, by_row, HIGHEST))
    if all_levels % 2:
        blocks.append(jnp.zeros((8, TABLE), F32))
    for pair in range(len(blocks) // 2):
        joined = jnp.concatenate([blocks[2 * pair], blocks[2 * pair + 1]], axis=1)[:heads]
        for d in range(table_ref.shape[0]):
            table_ref[d, pair * heads : (pair + 1) * heads, :] = joined


def final_kernel(cross_ref, inner_ref, key_ref, value_ref, dk_ref, dv_ref, grad_key_ref, grad_value_ref):
    heads = key_ref.shape[1] // CH
    spans = key_ref.shape[0] // CH
    for h in range(heads):
        cols = span_rows(h)
        cross = get_slices(cross_ref, h)
        for c in range(spans):
            rows = span_rows(c)
            state = cross if c == 1 else (inner_ref[cols, :] + cross.astype(F32)).astype(BF16)
            grad_key = dk_ref[rows, cols] + dot_nt(value_ref[rows, cols], state)
            grad_value = dv_ref[rows, cols] + dot_nn(key_ref[rows, cols], state)
            grad_key_ref[rows, cols] = grad_key.astype(BF16)
            grad_value_ref[rows, cols] = grad_value.astype(BF16)


def exchange(value, axis):
    return lax.all_to_all(value, axis, split_axis=0, concat_axis=0, tiled=True)


def body(queries, key_rows, value_rows, level_table, level_index, norm_gain, cotangent):
    tokens, width = queries.shape
    heads = level_table.shape[2]
    all_levels = level_table.shape[1]
    shards = lax.axis_size("seq")
    columns = lax.axis_size("head")
    levels = shards.bit_length() - 1
    height = heads * CH // shards
    own = tokens // columns

    cot = exchange(jnp.transpose(cotangent.reshape(own, columns, width), (1, 0, 2)), "head").reshape(tokens, width)
    gain = lax.dynamic_slice(norm_gain, (lax.axis_index("head") * width,), (width,)).reshape(1, width)
    table = jnp.transpose(level_table, (1, 0, 2)).reshape(all_levels * TABLE, heads)

    total, first = call(
        state_kernel,
        "span_states",
        (shaped((shards, height, CH), BF16), shaped((heads * CH, CH), BF16)),
        key_rows,
        value_rows,
    )
    slices = exchange(total, "seq")
    weights = call(weight_kernel, "level_weights", shaped((tokens, all_levels * heads), F32), level_index, table)
    near = call(
        near_kernel, "near_attention", shaped((tokens, width), F32), queries, key_rows, value_rows, first, weights
    )
    group_states = call(prefix_kernel, "prefix_states", shaped((shards, levels, height, CH), BF16), slices)
    states = exchange(group_states.reshape(shards, levels * height, CH), "seq").reshape(group_states.shape)
    attn, stat = call(
        far_kernel,
        "far_attention",
        (shaped((tokens, width), BF16), shaped((columns, 8, CH), F32)),
        near,
        queries,
        states,
        weights,
        cot,
        gain,
    )
    stats = exchange(stat, "head")
    grad, groups = call(
        grad_kernel,
        "attention_grad",
        (shaped((tokens, width), BF16), shaped((shards, levels, height, CH), BF16)),
        attn,
        stats,
        cot,
        gain,
        queries,
        weights,
    )
    group_slices = exchange(groups.reshape(shards, levels * height, CH), "seq").reshape(groups.shape)
    normed, gain_part = call(
        norm_kernel,
        "norm_output",
        (shaped((tokens, width), BF16), shaped((shards, 8, CH), F32)),
        attn,
        stats,
        cot,
        gain,
    )
    normed = exchange(normed.reshape(columns, own, width), "head")
    normed = jnp.transpose(normed, (1, 0, 2)).reshape(own, columns * width)
    gain_sum = jnp.sum(exchange(gain_part, "seq"), axis=0)
    gain_all = exchange(jnp.broadcast_to(gain_sum[None], (columns, 8, CH)), "head")
    grad_gain = gain_all[:, :heads].reshape(columns * width)

    pairs = (all_levels + 1) // 2
    grad_query, near_dk, near_dv, inner, table_part, _ = call(
        back_kernel,
        "query_grad",
        (
            shaped((tokens, width), BF16),
            shaped((tokens, width), F32),
            shaped((tokens, width), F32),
            shaped((heads * CH, CH), F32),
            shaped((shards, pairs * heads, 2 * TABLE), F32),
            shaped((tokens, CH), F32),
        ),
        queries,
        key_rows,
        value_rows,
        grad,
        weights,
        states,
        first,
        level_index,
    )
    table_sum = jnp.sum(exchange(table_part, "seq"), axis=0)
    table_sum = table_sum.reshape(pairs, heads, 2, TABLE).transpose(3, 0, 2, 1)
    grad_table = table_sum.reshape(TABLE, 2 * pairs, heads)[:, :all_levels]

    key_slices = call(suffix_kernel, "suffix_states", shaped((shards, height, CH), BF16), group_slices)
    cross = exchange(key_slices, "seq")
    grad_key, grad_value = call(
        final_kernel,
        "key_value_grad",
        (shaped((tokens, width), BF16), shaped((tokens, width), BF16)),
        cross,
        inner,
        key_rows,
        value_rows,
        near_dk,
        near_dv,
    )
    return normed, grad_query, grad_key, grad_value, grad_table, grad_gain


def solution(mesh):
    placed = (
        P("seq", "head"),
        P("seq", "head"),
        P("seq", "head"),
        P(None, None, "head"),
        P("seq", None),
        P(),
        P(("seq", "head"), None),
    )
    return jax.shard_map(
        body,
        mesh=mesh,
        in_specs=placed,
        out_specs=(
            P(("seq", "head"), None),
            P("seq", "head"),
            P("seq", "head"),
            P("seq", "head"),
            P(None, None, "head"),
            P(),
        ),
        check_vma=False,
    )
```

```python
import jax
import jax.numpy as jnp
from jax import lax
from jax.experimental import pallas as pl
from jax.experimental.pallas import tpu as pltpu
from jax.sharding import PartitionSpec as P

CH = 128
TABLE = 64
EPSILON = 1e-06
HIGHEST = lax.Precision.HIGHEST
F32 = jnp.float32
BF16 = jnp.bfloat16
INTERPRET = False


def call(kernel, out_shape, *operands):
    whole = pl.BlockSpec(memory_space=pltpu.VMEM)
    scalar = pl.BlockSpec(memory_space=pltpu.SMEM)
    return pl.pallas_call(
        kernel,
        out_shape=out_shape,
        in_specs=[scalar if operand.ndim == 1 else whole for operand in operands],
        interpret=INTERPRET,
        compiler_params=pltpu.CompilerParams(vmem_limit_bytes=48 * 1024 * 1024),
    )(*operands)


def shaped(shape, dtype):
    return jax.ShapeDtypeStruct(shape, dtype)


def dot_nn(a, b, precision=None):
    return lax.dot_general(a, b, (((1,), (0,)), ((), ())), precision=precision, preferred_element_type=F32)


def dot_nt(a, b):
    return lax.dot_general(a, b, (((1,), (1,)), ((), ())), preferred_element_type=F32)


def dot_tn(a, b, precision=None):
    return lax.dot_general(a, b, (((0,), (0,)), ((), ())), precision=precision, preferred_element_type=F32)


def causal_mask():
    rows = lax.broadcasted_iota(jnp.int32, (CH, CH), 0)
    cols = lax.broadcasted_iota(jnp.int32, (CH, CH), 1)
    return cols <= rows


def span_rows(c):
    return slice(c * CH, (c + 1) * CH)


def to_row(tile):
    return jnp.sum(tile.T, axis=0, keepdims=True)


def to_columns(row):
    return jnp.broadcast_to(row, (CH, CH)).T


def put_slices(ref, value, head, height, level=0):
    per_head = CH // height
    pieces = value.astype(BF16).reshape(per_head, height, value.shape[1])
    ref[head * per_head : (head + 1) * per_head, level * height : (level + 1) * height, :] = pieces


def get_slices(ref, head, height, level=0):
    per_head = CH // height
    pieces = ref[head * per_head : (head + 1) * per_head, level * height : (level + 1) * height, :]
    return pieces.reshape(CH, ref.shape[2])


def height_of(heads, ref):
    return heads * CH // ref.shape[0]


def split_pair(value):
    high = value.astype(BF16)
    return high, (value - high.astype(F32)).astype(BF16)


def state_kernel(key_ref, value_ref, total_ref, first_ref):
    heads = key_ref.shape[1] // CH
    for h in range(heads):
        cols = span_rows(h)
        first = dot_tn(key_ref[0:CH, cols], value_ref[0:CH, cols])
        second = dot_tn(key_ref[CH : 2 * CH, cols], value_ref[CH : 2 * CH, cols])
        first_ref[cols, :] = first.astype(BF16)
        put_slices(total_ref, first + second, h, total_ref.shape[1])


def prefix_kernel(in_ref, out_ref):
    shards, height = in_ref.shape[0], in_ref.shape[1]
    levels = out_ref.shape[1] // height
    sums = [in_ref[s].astype(F32) for s in range(shards)]
    zero = jnp.zeros(in_ref.shape[1:], BF16)
    for level in range(levels):
        rounded = [s.astype(BF16) for s in sums]
        for t in range(shards):
            group = t >> level
            out_ref[t, level * height : (level + 1) * height, :] = rounded[group - 1] if group & 1 else zero
        sums = [sums[2 * i] + sums[2 * i + 1] for i in range(len(sums) // 2)]


def suffix_kernel(place_ref, in_ref, table_ref, out_ref, gain_ref):
    shards = in_ref.shape[0]
    height = out_ref.shape[1] - table_ref.shape[0]
    levels = shards.bit_length() - 1
    rows = (in_ref.shape[1] - levels * height) // 2
    start = levels * height
    gain = in_ref[0, start : start + 2 * rows, :].astype(F32)
    for s in range(1, shards):
        gain = gain + in_ref[s, start : start + 2 * rows, :].astype(F32)
    gain = gain[:rows] + gain[rows:]
    for spot in range(gain_ref.shape[0] // rows):
        gain_ref[spot * rows : (spot + 1) * rows, :] = jnp.where(place_ref[0] == spot, gain, 0.0)
    carried = [None]
    for level in range(levels - 1, -1, -1):
        size = 1 << level
        groups = shards >> level
        below = []
        for g in range(groups):
            base = carried[g >> 1]
            if g & 1 == 0:
                total = None
                for s in range((g + 1) * size, (g + 2) * size):
                    piece = in_ref[s, level * height : (level + 1) * height, :].astype(F32)
                    total = piece if total is None else total + piece
                base = total if base is None else base + total
            below.append(base)
        carried = below
    zero = jnp.zeros((height, CH), F32)
    table = table_ref[...]
    for t in range(shards):
        value = zero if carried[t] is None else carried[t]
        out_ref[t, 0:height, :] = value.astype(BF16)
        out_ref[t, height:, :] = table


def onehot_of(index_ref, level):
    tokens = index_ref.shape[1]
    entry = lax.broadcasted_iota(jnp.int32, (TABLE, tokens), 0)
    return (index_ref[level : level + 1, :] == entry).astype(F32)


def weight_kernel(index_ref, table_ref, weight_ref):
    levels, tokens = index_ref.shape
    heads = table_ref.shape[1]
    rows = [dot_nn(table_ref[level], onehot_of(index_ref, level), HIGHEST) for level in range(levels)]
    rows.append(jnp.zeros((CH - levels * heads, tokens), F32))
    weight_ref[...] = jnp.concatenate(rows, axis=0).T


def near_kernel(query_ref, key_ref, value_ref, first_ref, weight_ref, out_ref):
    heads = query_ref.shape[1] // CH
    spans = query_ref.shape[0] // CH
    causal = causal_mask()
    for c in range(spans):
        rows = span_rows(c)
        for h in range(heads):
            cols = span_rows(h)
            query = query_ref[rows, cols]
            scores = jnp.where(causal, dot_nt(query, key_ref[rows, cols]), 0.0).astype(BF16)
            near = weight_ref[rows, h : h + 1] * dot_nn(scores, value_ref[rows, cols])
            if c == 1:
                near = near + weight_ref[rows, heads + h : heads + h + 1] * dot_nn(query, first_ref[cols, :])
            out_ref[rows, cols] = near


def spread_kernel(place_ref, in_ref, out_ref):
    width = out_ref.shape[2]
    for column in range(out_ref.shape[0]):
        out_ref[column ^ place_ref[0]] = in_ref[:, column * width : (column + 1) * width]


def collect_kernel(place_ref, in_ref, out_ref):
    width = in_ref.shape[2]
    for column in range(in_ref.shape[0]):
        out_ref[:, column * width : (column + 1) * width] = in_ref[column ^ place_ref[0]]


def span_block(place_ref, ref, c, cols):
    own = ref.shape[1]
    count = CH // own
    pieces = [ref[(c * count + i) ^ place_ref[0], :, cols] for i in range(count)]
    return jnp.concatenate(pieces, axis=0)


def far_kernel(place_ref, near_ref, query_ref, state_ref, weight_ref, cot_ref, gain_ref, attn_ref, stat_ref):
    heads = query_ref.shape[1] // CH
    spans = query_ref.shape[0] // CH
    height = height_of(heads, state_ref)
    levels = state_ref.shape[1] // height
    stats = []
    for c in range(spans):
        rows = span_rows(c)
        squares = jnp.zeros((CH, CH), F32)
        along = jnp.zeros((CH, CH), F32)
        for h in range(heads):
            cols = span_rows(h)
            query = query_ref[rows, cols]
            total = near_ref[rows, cols]
            for level in range(levels):
                spot = (level + 2) * heads + h
                total = total + weight_ref[rows, spot : spot + 1] * dot_nn(query, get_slices(state_ref, h, height, level))
            attn = total.astype(BF16)
            attn_ref[rows, cols] = attn
            attn_f = attn.astype(F32)
            scaled = span_block(place_ref, cot_ref, c, cols).astype(F32) * gain_ref[:, cols]
            squares = squares + attn_f * attn_f
            along = along + scaled * attn_f
        stats.append(to_row(squares))
        stats.append(to_row(along))
    block = jnp.concatenate(stats + [jnp.zeros((8 - len(stats), CH), F32)], axis=0)
    for d in range(stat_ref.shape[0]):
        stat_ref[d] = block


def norm_columns(stat_ref, features, c):
    total = stat_ref[0]
    for d in range(1, stat_ref.shape[0]):
        total = total + stat_ref[d]
    inv_rms = lax.rsqrt(total[2 * c : 2 * c + 1, :] / features + EPSILON)
    mean = total[2 * c + 1 : 2 * c + 2, :] * inv_rms / features
    return to_columns(inv_rms), to_columns(mean)


def grad_kernel(place_ref, attn_ref, stat_ref, cot_ref, gain_ref, query_ref, weight_ref, grad_ref, group_ref):
    heads = query_ref.shape[1] // CH
    spans = query_ref.shape[0] // CH
    height = height_of(heads, group_ref)
    levels = group_ref.shape[1] // height
    start = levels * height
    features = float(stat_ref.shape[0] * attn_ref.shape[1])
    norms = [norm_columns(stat_ref, features, c) for c in range(spans)]
    gain_parts = []
    for h in range(heads):
        cols = span_rows(h)
        parts = [[] for _ in range(levels)]
        gain_part = jnp.zeros((1, CH), F32)
        for c in range(spans):
            rows = span_rows(c)
            inv_rms, mean = norms[c]
            unit = attn_ref[rows, cols].astype(F32) * inv_rms
            cot = span_block(place_ref, cot_ref, c, cols).astype(F32)
            gain_part = gain_part + jnp.sum(cot * unit, axis=0, keepdims=True)
            scaled = cot * gain_ref[:, cols]
            grad = ((scaled - unit * mean) * inv_rms).astype(BF16)
            grad_ref[rows, cols] = grad
            grad_f = grad.astype(F32)
            for level in range(levels):
                spot = (level + 2) * heads + h
                parts[level].append((weight_ref[rows, spot : spot + 1] * grad_f).astype(BF16))
        query = query_ref[:, cols]
        for level in range(levels):
            put_slices(group_ref, dot_tn(query, jnp.concatenate(parts[level], axis=0)), h, height, level)
        gain_parts.append(gain_part)
    high, low = split_pair(jnp.concatenate(gain_parts, axis=0))
    block = jnp.concatenate([high, low], axis=0)
    for d in range(group_ref.shape[0]):
        group_ref[d, start:, :] = block


def norm_kernel(place_ref, attn_ref, stat_ref, gain_ref, normed_ref):
    heads = attn_ref.shape[1] // CH
    spans = attn_ref.shape[0] // CH
    features = float(stat_ref.shape[0] * attn_ref.shape[1])
    own = normed_ref.shape[1]
    for c in range(spans):
        rows = span_rows(c)
        inv_rms, _ = norm_columns(stat_ref, features, c)
        for h in range(heads):
            cols = span_rows(h)
            unit = attn_ref[rows, cols].astype(F32) * inv_rms
            normed = (unit * gain_ref[:, cols]).astype(BF16)
            for i in range(CH // own):
                normed_ref[(c * (CH // own) + i) ^ place_ref[0], :, cols] = normed[i * own : (i + 1) * own]


def back_kernel(
    query_ref, key_ref, value_ref, grad_ref, weight_ref, state_ref, first_ref, index_ref,
    dq_ref, dk_ref, dv_ref, inner_ref, table_ref, gw_ref,
):
    heads = query_ref.shape[1] // CH
    spans = query_ref.shape[0] // CH
    height = height_of(heads, state_ref)
    levels = state_ref.shape[1] // height
    all_levels = levels + 2
    causal = causal_mask()
    gw_ref[...] = jnp.zeros(gw_ref.shape, F32)
    for c in range(spans):
        rows = span_rows(c)
        for h in range(heads):
            cols = span_rows(h)
            query = query_ref[rows, cols]
            query_f = query.astype(F32)
            key = key_ref[rows, cols]
            grad = grad_ref[rows, cols]
            first_weight = weight_ref[rows, h : h + 1]
            scores = jnp.where(causal, dot_nt(query, key), 0.0)
            along = jnp.where(causal, dot_nt(grad, value_ref[rows, cols]), 0.0)
            gw_ref[rows, h : h + 1] = jnp.sum(scores.astype(BF16).astype(F32) * along, axis=1, keepdims=True)
            grad_scores = (along * first_weight).astype(BF16)
            weighted = (scores * first_weight).astype(BF16)
            dq = dot_nn(grad_scores, key)
            dk_ref[rows, cols] = dot_tn(grad_scores, query)
            dv_ref[rows, cols] = dot_tn(weighted, grad)
            if c == 1:
                spot = heads + h
                weight = weight_ref[rows, spot : spot + 1]
                far = dot_nt(grad, first_ref[cols, :])
                gw_ref[rows, spot : spot + 1] = jnp.sum(query_f * far, axis=1, keepdims=True)
                dq = dq + weight * far
                inner_ref[cols, :] = dot_tn(query, (weight * grad.astype(F32)).astype(BF16))
            for level in range(levels):
                spot = (level + 2) * heads + h
                far = dot_nt(grad, get_slices(state_ref, h, height, level))
                gw_ref[rows, spot : spot + 1] = jnp.sum(query_f * far, axis=1, keepdims=True)
                dq = dq + weight_ref[rows, spot : spot + 1] * far
            dq_ref[rows, cols] = dq.astype(BF16)
    grads = gw_ref[...].T
    blocks = []
    for level in range(all_levels):
        by_row = lax.dot_general(
            grads, onehot_of(index_ref, level), (((1,), (1,)), ((), ())), precision=HIGHEST, preferred_element_type=F32
        )
        blocks.append(by_row[level * heads : (level + 1) * heads])
    if all_levels % 2:
        blocks.append(jnp.zeros((heads, TABLE), F32))
    joined = [
        jnp.concatenate([blocks[2 * pair], blocks[2 * pair + 1]], axis=1) for pair in range(len(blocks) // 2)
    ]
    high, low = split_pair(jnp.concatenate(joined, axis=0))
    table_ref[...] = jnp.concatenate([high, low], axis=0)


def final_kernel(
    cross_ref, inner_ref, key_ref, value_ref, dk_ref, dv_ref, grad_key_ref, grad_value_ref, table_ref
):
    heads = key_ref.shape[1] // CH
    spans = key_ref.shape[0] // CH
    height = height_of(heads, cross_ref)
    half = (cross_ref.shape[1] - height) // 2
    total = cross_ref[0, height:, :].astype(F32)
    for s in range(1, cross_ref.shape[0]):
        total = total + cross_ref[s, height:, :].astype(F32)
    total = total[:half] + total[half:]
    for level in range(table_ref.shape[0]):
        top, left = (level // 2) * heads, (level % 2) * TABLE
        table_ref[level] = total[top : top + heads, left : left + TABLE]
    for h in range(heads):
        cols = span_rows(h)
        cross = get_slices(cross_ref, h, height)
        for c in range(spans):
            rows = span_rows(c)
            state = cross if c == 1 else (inner_ref[cols, :] + cross.astype(F32)).astype(BF16)
            grad_key = dk_ref[rows, cols] + dot_nt(value_ref[rows, cols], state)
            grad_value = dv_ref[rows, cols] + dot_nn(key_ref[rows, cols], state)
            grad_key_ref[rows, cols] = grad_key.astype(BF16)
            grad_value_ref[rows, cols] = grad_value.astype(BF16)


def exchange(value, axis):
    return lax.all_to_all(value, axis, split_axis=0, concat_axis=0, tiled=True)


def swapped(value, axis, bit):
    pairs = [(source, source ^ (1 << bit)) for source in range(lax.axis_size(axis))]
    return lax.ppermute(value, axis, pairs)


def gathered(slots):
    arrays = []
    for array, _ in slots:
        if not any(array is other for other in arrays):
            arrays.append(array)
    places = [(next(i for i, other in enumerate(arrays) if other is array), row) for array, row in slots]

    def pack_kernel(*refs):
        for spot, (source, row) in enumerate(places):
            refs[-1][spot] = refs[source][row]

    return call(pack_kernel, shaped((len(slots),) + arrays[0].shape[1:], arrays[0].dtype), *arrays)


def cube_exchange(value, axis):
    count = value.shape[0]
    slots = [(value, row) for row in range(count)]
    for bit in range(count.bit_length() - 2, -1, -1):
        moving = [row for row in range(count) if row >> bit & 1]
        received = swapped(gathered([slots[row] for row in moving]), axis, bit)
        for spot, row in enumerate(moving):
            slots[row] = (received, spot)
    return gathered(slots)


def body(queries, key_rows, value_rows, level_table, level_index, norm_gain, cotangent):
    tokens, width = queries.shape
    heads = level_table.shape[2]
    all_levels = level_table.shape[1]
    shards = lax.axis_size("seq")
    columns = lax.axis_size("head")
    levels = shards.bit_length() - 1
    height = heads * CH // shards
    own = tokens // columns
    pairs = (all_levels + 1) // 2
    place = lax.axis_index("head")
    spot = place.reshape(1)

    total, first = call(
        state_kernel, (shaped((shards, height, CH), BF16), shaped((heads * CH, CH), BF16)), key_rows, value_rows
    )
    slices = exchange(total, "seq")
    cot = call(spread_kernel, shaped((columns, own, width), BF16), spot, cotangent)
    cot = cube_exchange(cot, "head")
    gain = lax.dynamic_slice(norm_gain, (place * width,), (width,)).reshape(1, width)
    table = jnp.transpose(level_table, (1, 2, 0))
    index = jnp.transpose(level_index)
    weights = call(weight_kernel, shaped((tokens, CH), F32), index, table)
    near = call(near_kernel, shaped((tokens, width), F32), queries, key_rows, value_rows, first, weights)
    group_states = call(prefix_kernel, shaped((shards, levels * height, CH), BF16), slices)
    states = exchange(group_states, "seq")
    attn, stat = call(
        far_kernel,
        (shaped((tokens, width), BF16), shaped((columns, 8, CH), F32)),
        spot,
        near,
        queries,
        states,
        weights,
        cot,
        gain,
    )
    stats = exchange(stat, "head")
    grad, groups = call(
        grad_kernel,
        (shaped((tokens, width), BF16), shaped((shards, levels * height + 2 * heads, CH), BF16)),
        spot,
        attn,
        stats,
        cot,
        gain,
        queries,
        weights,
    )
    group_slices = exchange(groups, "seq")
    normed = call(norm_kernel, shaped((columns, own, width), BF16), spot, attn, stats, gain)
    normed = cube_exchange(normed, "head")
    normed = call(collect_kernel, shaped((own, columns * width), BF16), spot, normed)
    grad_query, near_dk, near_dv, inner, table_part, _ = call(
        back_kernel,
        (
            shaped((tokens, width), BF16),
            shaped((tokens, width), F32),
            shaped((tokens, width), F32),
            shaped((heads * CH, CH), F32),
            shaped((2 * pairs * heads, 2 * TABLE), BF16),
            shaped((tokens, CH), F32),
        ),
        queries,
        key_rows,
        value_rows,
        grad,
        weights,
        states,
        first,
        index,
    )
    key_slices, gain_sum = call(
        suffix_kernel,
        (
            shaped((shards, height + 2 * pairs * heads, CH), BF16),
            shaped((columns * heads, CH), F32),
        ),
        spot,
        group_slices,
        table_part,
    )
    cross = exchange(key_slices, "seq")
    for bit in range(columns.bit_length() - 1):
        gain_sum = gain_sum + swapped(gain_sum, "head", bit)
    grad_key, grad_value, table_sum = call(
        final_kernel,
        (
            shaped((tokens, width), BF16),
            shaped((tokens, width), BF16),
            shaped((all_levels, heads, TABLE), F32),
        ),
        cross,
        inner,
        key_rows,
        value_rows,
        near_dk,
        near_dv,
    )
    grad_table = jnp.transpose(table_sum, (2, 0, 1))
    return normed, grad_query, grad_key, grad_value, grad_table, gain_sum.reshape(columns * width)


def solution(mesh):
    placed = (
        P("seq", "head"),
        P("seq", "head"),
        P("seq", "head"),
        P(None, None, "head"),
        P("seq", None),
        P(),
        P(("seq", "head"), None),
    )
    return jax.shard_map(
        body,
        mesh=mesh,
        in_specs=placed,
        out_specs=(
            P(("seq", "head"), None),
            P("seq", "head"),
            P("seq", "head"),
            P("seq", "head"),
            P(None, None, "head"),
            P(),
        ),
        check_vma=False,
    )
```

```python
import jax
import jax.numpy as jnp
from jax import lax
from jax.experimental import pallas as pl
from jax.experimental.pallas import tpu as pltpu
from jax.sharding import PartitionSpec as P

CH = 128
TABLE = 64
EPSILON = 1e-06
HIGHEST = lax.Precision.HIGHEST
F32 = jnp.float32
BF16 = jnp.bfloat16
INTERPRET = False


def call(kernel, out_shape, *operands):
    whole = pl.BlockSpec(memory_space=pltpu.VMEM)
    scalar = pl.BlockSpec(memory_space=pltpu.SMEM)
    return pl.pallas_call(
        kernel,
        out_shape=out_shape,
        in_specs=[scalar if operand.ndim == 1 else whole for operand in operands],
        interpret=INTERPRET,
        compiler_params=pltpu.CompilerParams(vmem_limit_bytes=48 * 1024 * 1024),
    )(*operands)


def shaped(shape, dtype):
    return jax.ShapeDtypeStruct(shape, dtype)


def dot_nn(a, b, precision=None):
    return lax.dot_general(a, b, (((1,), (0,)), ((), ())), precision=precision, preferred_element_type=F32)


def dot_nt(a, b):
    return lax.dot_general(a, b, (((1,), (1,)), ((), ())), preferred_element_type=F32)


def dot_tn(a, b, precision=None):
    return lax.dot_general(a, b, (((0,), (0,)), ((), ())), precision=precision, preferred_element_type=F32)


def causal_mask():
    rows = lax.broadcasted_iota(jnp.int32, (CH, CH), 0)
    cols = lax.broadcasted_iota(jnp.int32, (CH, CH), 1)
    return cols <= rows


def span_rows(c):
    return slice(c * CH, (c + 1) * CH)


def put_slices(ref, value, head, height, level=0):
    per_head = CH // height
    pieces = value.astype(BF16).reshape(per_head, height, value.shape[1])
    ref[head * per_head : (head + 1) * per_head, level * height : (level + 1) * height, :] = pieces


def get_slices(ref, head, height, level=0):
    per_head = CH // height
    pieces = ref[head * per_head : (head + 1) * per_head, level * height : (level + 1) * height, :]
    return pieces.reshape(CH, ref.shape[2])


def height_of(heads, ref):
    return heads * CH // ref.shape[0]


def split_pair(value):
    high = value.astype(BF16)
    return high, (value - high.astype(F32)).astype(BF16)


def state_kernel(key_ref, value_ref, total_ref, first_ref):
    heads = key_ref.shape[1] // CH
    for h in range(heads):
        cols = span_rows(h)
        first = dot_tn(key_ref[0:CH, cols], value_ref[0:CH, cols])
        second = dot_tn(key_ref[CH : 2 * CH, cols], value_ref[CH : 2 * CH, cols])
        first_ref[cols, :] = first.astype(BF16)
        put_slices(total_ref, first + second, h, total_ref.shape[1])


def prefix_kernel(in_ref, out_ref):
    shards, height = in_ref.shape[0], in_ref.shape[1]
    levels = out_ref.shape[1] // height
    sums = [in_ref[s].astype(F32) for s in range(shards)]
    zero = jnp.zeros(in_ref.shape[1:], BF16)
    for level in range(levels):
        rounded = [s.astype(BF16) for s in sums]
        for t in range(shards):
            group = t >> level
            out_ref[t, level * height : (level + 1) * height, :] = rounded[group - 1] if group & 1 else zero
        sums = [sums[2 * i] + sums[2 * i + 1] for i in range(len(sums) // 2)]


def suffix_kernel(in_ref, table_ref, out_ref):
    shards = in_ref.shape[0]
    levels = shards.bit_length() - 1
    height = in_ref.shape[1] // (8 * levels) * 8
    start = levels * height
    table_rows = table_ref.shape[0]
    rows = out_ref.shape[1] - height - table_rows
    gain = in_ref[0, start:, :].astype(F32)
    for s in range(1, shards):
        gain = gain + in_ref[s, start:, :].astype(F32)
    gain = (gain[:rows] + gain[rows : 2 * rows]).astype(BF16)
    tail = jnp.concatenate([table_ref[...], gain], axis=0)
    carried = [None]
    for level in range(levels - 1, -1, -1):
        size = 1 << level
        groups = shards >> level
        below = []
        for g in range(groups):
            base = carried[g >> 1]
            if g & 1 == 0:
                total = None
                for s in range((g + 1) * size, (g + 2) * size):
                    piece = in_ref[s, level * height : (level + 1) * height, :].astype(F32)
                    total = piece if total is None else total + piece
                base = total if base is None else base + total
            below.append(base)
        carried = below
    zero = jnp.zeros((height, CH), F32)
    for t in range(shards):
        value = zero if carried[t] is None else carried[t]
        out_ref[t, 0:height, :] = value.astype(BF16)
        out_ref[t, height:, :] = tail


def onehot_of(index_ref, level):
    tokens = index_ref.shape[1]
    entry = lax.broadcasted_iota(jnp.int32, (TABLE, tokens), 0)
    return (index_ref[level : level + 1, :] == entry).astype(F32)


def weight_kernel(index_ref, table_ref, weight_ref):
    levels, tokens = index_ref.shape
    heads = table_ref.shape[1]
    rows = [dot_nn(table_ref[level], onehot_of(index_ref, level), HIGHEST) for level in range(levels)]
    rows.append(jnp.zeros((CH - levels * heads, tokens), F32))
    weight_ref[...] = jnp.concatenate(rows, axis=0).T


def near_kernel(query_ref, key_ref, value_ref, first_ref, weight_ref, out_ref):
    heads = query_ref.shape[1] // CH
    spans = query_ref.shape[0] // CH
    causal = causal_mask()
    for c in range(spans):
        rows = span_rows(c)
        for h in range(heads):
            cols = span_rows(h)
            query = query_ref[rows, cols]
            scores = jnp.where(causal, dot_nt(query, key_ref[rows, cols]), 0.0).astype(BF16)
            near = weight_ref[rows, h : h + 1] * dot_nn(scores, value_ref[rows, cols])
            if c == 1:
                near = near + weight_ref[rows, heads + h : heads + h + 1] * dot_nn(query, first_ref[cols, :])
            out_ref[rows, cols] = near


def far_kernel(near_ref, query_ref, state_ref, weight_ref, attn_ref):
    heads = query_ref.shape[1] // CH
    spans = query_ref.shape[0] // CH
    height = height_of(heads, state_ref)
    levels = state_ref.shape[1] // height
    for c in range(spans):
        rows = span_rows(c)
        for h in range(heads):
            cols = span_rows(h)
            query = query_ref[rows, cols]
            total = near_ref[rows, cols]
            for level in range(levels):
                spot = (level + 2) * heads + h
                total = total + weight_ref[rows, spot : spot + 1] * dot_nn(query, get_slices(state_ref, h, height, level))
            attn_ref[rows, cols] = total.astype(BF16)


def norm_kernel(attn_ref, cot_ref, gain_ref, normed_ref, grad_ref):
    columns, own, width = attn_ref.shape
    features = float(columns * width)
    squares = jnp.zeros((own, width), F32)
    along = jnp.zeros((own, width), F32)
    for d in range(columns):
        cols = slice(d * width, (d + 1) * width)
        attn = attn_ref[d].astype(F32)
        squares = squares + attn * attn
        along = along + cot_ref[:, cols].astype(F32) * gain_ref[:, cols] * attn
    inv_rms = lax.rsqrt(jnp.sum(squares, axis=1, keepdims=True) / features + EPSILON)
    mean = jnp.sum(along, axis=1, keepdims=True) * inv_rms / features
    parts = []
    for d in range(columns):
        cols = slice(d * width, (d + 1) * width)
        cot = cot_ref[:, cols].astype(F32)
        unit = attn_ref[d].astype(F32) * inv_rms
        normed_ref[:, cols] = (unit * gain_ref[:, cols]).astype(BF16)
        grad_ref[d, 0:own, :] = ((cot * gain_ref[:, cols] - unit * mean) * inv_rms).astype(BF16)
        parts.append(jnp.sum(cot * unit, axis=0, keepdims=True))
    block = jnp.concatenate(parts, axis=0).astype(BF16)
    for d in range(columns):
        grad_ref[d, own:, :] = block


def grad_kernel(head_ref, query_ref, weight_ref, grad_ref, group_ref):
    columns = head_ref.shape[0]
    own = head_ref.shape[1] - columns
    heads = query_ref.shape[1] // CH
    shards = group_ref.shape[0]
    height = height_of(heads, group_ref)
    levels = group_ref.shape[1] // height
    start = levels * height
    for d in range(columns):
        grad_ref[d * own : (d + 1) * own, :] = head_ref[d, 0:own, :]
    for h in range(heads):
        cols = span_rows(h)
        grad_f = grad_ref[:, cols].astype(F32)
        query = query_ref[:, cols]
        for level in range(levels):
            spot = (level + 2) * heads + h
            scaled = (weight_ref[:, spot : spot + 1] * grad_f).astype(BF16)
            put_slices(group_ref, dot_tn(query, scaled), h, height, level)
    gain = head_ref[0, own:, :].astype(F32)
    for d in range(1, columns):
        gain = gain + head_ref[d, own:, :].astype(F32)
    rows = columns * heads // shards
    extra = group_ref.shape[1] - start
    for s in range(shards):
        spots = range(s * rows, (s + 1) * rows)
        picked = [gain[i // heads : i // heads + 1, span_rows(i % heads)] for i in spots]
        high, low = split_pair(jnp.concatenate(picked, axis=0))
        fill = jnp.zeros((extra - 2 * rows, CH), BF16)
        group_ref[s, start:, :] = jnp.concatenate([high, low, fill], axis=0)


def back_kernel(
    query_ref, key_ref, value_ref, grad_ref, weight_ref, state_ref, first_ref, index_ref,
    dq_ref, dk_ref, dv_ref, inner_ref, table_ref, gw_ref,
):
    heads = query_ref.shape[1] // CH
    spans = query_ref.shape[0] // CH
    height = height_of(heads, state_ref)
    levels = state_ref.shape[1] // height
    all_levels = levels + 2
    causal = causal_mask()
    gw_ref[...] = jnp.zeros(gw_ref.shape, F32)
    for c in range(spans):
        rows = span_rows(c)
        for h in range(heads):
            cols = span_rows(h)
            query = query_ref[rows, cols]
            query_f = query.astype(F32)
            key = key_ref[rows, cols]
            grad = grad_ref[rows, cols]
            first_weight = weight_ref[rows, h : h + 1]
            scores = jnp.where(causal, dot_nt(query, key), 0.0)
            along = jnp.where(causal, dot_nt(grad, value_ref[rows, cols]), 0.0)
            gw_ref[rows, h : h + 1] = jnp.sum(scores.astype(BF16).astype(F32) * along, axis=1, keepdims=True)
            grad_scores = (along * first_weight).astype(BF16)
            weighted = (scores * first_weight).astype(BF16)
            dq = dot_nn(grad_scores, key)
            dk_ref[rows, cols] = dot_tn(grad_scores, query)
            dv_ref[rows, cols] = dot_tn(weighted, grad)
            if c == 1:
                spot = heads + h
                weight = weight_ref[rows, spot : spot + 1]
                far = dot_nt(grad, first_ref[cols, :])
                gw_ref[rows, spot : spot + 1] = jnp.sum(query_f * far, axis=1, keepdims=True)
                dq = dq + weight * far
                inner_ref[cols, :] = dot_tn(query, (weight * grad.astype(F32)).astype(BF16))
            for level in range(levels):
                spot = (level + 2) * heads + h
                far = dot_nt(grad, get_slices(state_ref, h, height, level))
                gw_ref[rows, spot : spot + 1] = jnp.sum(query_f * far, axis=1, keepdims=True)
                dq = dq + weight_ref[rows, spot : spot + 1] * far
            dq_ref[rows, cols] = dq.astype(BF16)
    grads = gw_ref[...].T
    blocks = []
    for level in range(all_levels):
        by_row = lax.dot_general(
            grads, onehot_of(index_ref, level), (((1,), (1,)), ((), ())), precision=HIGHEST, preferred_element_type=F32
        )
        blocks.append(by_row[level * heads : (level + 1) * heads])
    joined = [jnp.concatenate(blocks[2 * pair : 2 * pair + 2], axis=1) for pair in range(all_levels // 2)]
    for h in range(0, heads if all_levels % 2 else 0, 2):
        joined.append(jnp.concatenate([blocks[-1][h : h + 1], blocks[-1][h + 1 : h + 2]], axis=1))
    table_ref[...] = jnp.concatenate(joined, axis=0).astype(BF16)


def final_kernel(
    cross_ref, inner_ref, key_ref, value_ref, dk_ref, dv_ref, grad_key_ref, grad_value_ref, table_ref, gain_ref
):
    heads = key_ref.shape[1] // CH
    spans = key_ref.shape[0] // CH
    shards = cross_ref.shape[0]
    height = height_of(heads, cross_ref)
    rows = gain_ref.shape[0] // shards
    table_end = cross_ref.shape[1] - height - rows
    total = None
    for s in range(shards):
        tail = cross_ref[s, height:, :].astype(F32)
        total = tail if total is None else total + tail
        gain_ref[s * rows : (s + 1) * rows, :] = tail[table_end:]
    all_levels = table_ref.shape[0]
    for level in range(all_levels):
        if level == all_levels - 1 and all_levels % 2:
            base = (level // 2) * heads
            for h in range(heads):
                spot, left = base + h // 2, (h % 2) * TABLE
                table_ref[level, h : h + 1, :] = total[spot : spot + 1, left : left + TABLE]
        else:
            top, left = (level // 2) * heads, (level % 2) * TABLE
            table_ref[level] = total[top : top + heads, left : left + TABLE]
    for h in range(heads):
        cols = span_rows(h)
        cross = get_slices(cross_ref, h, height)
        for c in range(spans):
            rows = span_rows(c)
            state = cross if c == 1 else (inner_ref[cols, :] + cross.astype(F32)).astype(BF16)
            grad_key = dk_ref[rows, cols] + dot_nt(value_ref[rows, cols], state)
            grad_value = dv_ref[rows, cols] + dot_nn(key_ref[rows, cols], state)
            grad_key_ref[rows, cols] = grad_key.astype(BF16)
            grad_value_ref[rows, cols] = grad_value.astype(BF16)


def exchange(value, axis):
    return lax.all_to_all(value, axis, split_axis=0, concat_axis=0, tiled=True)


def body(queries, key_rows, value_rows, level_table, level_index, norm_gain, cotangent):
    tokens, width = queries.shape
    heads = level_table.shape[2]
    all_levels = level_table.shape[1]
    shards = lax.axis_size("seq")
    columns = lax.axis_size("head")
    levels = shards.bit_length() - 1
    height = heads * CH // shards
    own = tokens // columns
    table_rows = all_levels * heads * TABLE // CH
    gain_rows = columns * heads // shards

    total, first = call(
        state_kernel, (shaped((shards, height, CH), BF16), shaped((heads * CH, CH), BF16)), key_rows, value_rows
    )
    slices = exchange(total, "seq")
    gain = norm_gain.reshape(1, columns * width)
    table = jnp.transpose(level_table, (1, 2, 0))
    index = jnp.transpose(level_index)
    weights = call(weight_kernel, shaped((tokens, CH), F32), index, table)
    near = call(near_kernel, shaped((tokens, width), F32), queries, key_rows, value_rows, first, weights)
    group_states = call(prefix_kernel, shaped((shards, levels * height, CH), BF16), slices)
    states = exchange(group_states, "seq")
    attn = call(far_kernel, shaped((tokens, width), BF16), near, queries, states, weights)
    token_attn = exchange(attn.reshape(columns, own, width), "head")
    normed, token_grad = call(
        norm_kernel,
        (shaped((own, columns * width), BF16), shaped((columns, own + columns, width), BF16)),
        token_attn,
        cotangent,
        gain,
    )
    head_grad = exchange(token_grad, "head")
    grad, groups = call(
        grad_kernel,
        (shaped((tokens, width), BF16), shaped((shards, levels * height + 8, CH), BF16)),
        head_grad,
        queries,
        weights,
    )
    group_slices = exchange(groups, "seq")
    grad_query, near_dk, near_dv, inner, table_part, _ = call(
        back_kernel,
        (
            shaped((tokens, width), BF16),
            shaped((tokens, width), F32),
            shaped((tokens, width), F32),
            shaped((heads * CH, CH), F32),
            shaped((table_rows, CH), BF16),
            shaped((tokens, CH), F32),
        ),
        queries,
        key_rows,
        value_rows,
        grad,
        weights,
        states,
        first,
        index,
    )
    key_slices = call(
        suffix_kernel, shaped((shards, height + table_rows + gain_rows, CH), BF16), group_slices, table_part
    )
    cross = exchange(key_slices, "seq")
    grad_key, grad_value, table_sum, gain_sum = call(
        final_kernel,
        (
            shaped((tokens, width), BF16),
            shaped((tokens, width), BF16),
            shaped((all_levels, heads, TABLE), F32),
            shaped((columns * heads, CH), F32),
        ),
        cross,
        inner,
        key_rows,
        value_rows,
        near_dk,
        near_dv,
    )
    grad_table = jnp.transpose(table_sum, (2, 0, 1))
    return normed, grad_query, grad_key, grad_value, grad_table, gain_sum.reshape(columns * width)


def solution(mesh):
    placed = (
        P("seq", "head"),
        P("seq", "head"),
        P("seq", "head"),
        P(None, None, "head"),
        P("seq", None),
        P(),
        P(("seq", "head"), None),
    )
    return jax.shard_map(
        body,
        mesh=mesh,
        in_specs=placed,
        out_specs=(
            P(("seq", "head"), None),
            P("seq", "head"),
            P("seq", "head"),
            P("seq", "head"),
            P(None, None, "head"),
            P(),
        ),
        check_vma=False,
    )
```

```python
import jax
import jax.numpy as jnp
from jax import lax
from jax.experimental import pallas as pl
from jax.experimental.pallas import tpu as pltpu
from jax.sharding import PartitionSpec as P

CH = 128
TABLE = 64
EPSILON = 1e-06
HIGHEST = lax.Precision.HIGHEST
F32 = jnp.float32
BF16 = jnp.bfloat16
INTERPRET = False
ROW_BITS = 2


def call(kernel, out_shape, *operands):
    whole = pl.BlockSpec(memory_space=pltpu.VMEM)
    scalar = pl.BlockSpec(memory_space=pltpu.SMEM)
    return pl.pallas_call(
        kernel,
        out_shape=out_shape,
        in_specs=[scalar if operand.ndim == 1 else whole for operand in operands],
        interpret=INTERPRET,
        compiler_params=pltpu.CompilerParams(vmem_limit_bytes=16 * 1024 * 1024),
    )(*operands)


def shaped(shape, dtype):
    return jax.ShapeDtypeStruct(shape, dtype)


def dot_nn(a, b, precision=None):
    return lax.dot_general(a, b, (((1,), (0,)), ((), ())), precision=precision, preferred_element_type=F32)


def dot_nt(a, b):
    return lax.dot_general(a, b, (((1,), (1,)), ((), ())), preferred_element_type=F32)


def dot_tn(a, b, precision=None):
    return lax.dot_general(a, b, (((0,), (0,)), ((), ())), precision=precision, preferred_element_type=F32)


def causal_mask():
    rows = lax.broadcasted_iota(jnp.int32, (CH, CH), 0)
    cols = lax.broadcasted_iota(jnp.int32, (CH, CH), 1)
    return cols <= rows


def span_rows(c):
    return slice(c * CH, (c + 1) * CH)


def put_slices(ref, value, head, height, level=0):
    per_head = CH // height
    pieces = value.astype(BF16).reshape(per_head, height, value.shape[1])
    ref[head * per_head : (head + 1) * per_head, level * height : (level + 1) * height, :] = pieces


def get_slices(ref, head, height, level=0):
    per_head = CH // height
    pieces = ref[head * per_head : (head + 1) * per_head, level * height : (level + 1) * height, :]
    return pieces.reshape(CH, ref.shape[2])


def height_of(heads, ref):
    return heads * CH // ref.shape[0]


def split_pair(value):
    high = value.astype(BF16)
    return high, (value - high.astype(F32)).astype(BF16)


def state_kernel(key_hbm, value_hbm, total_ref, first_ref, key_ref, value_ref, sems):
    key_copy = pltpu.make_async_copy(key_hbm, key_ref, sems.at[0])
    value_copy = pltpu.make_async_copy(value_hbm, value_ref, sems.at[1])
    key_copy.start()
    value_copy.start()
    key_copy.wait()
    value_copy.wait()
    heads = key_ref.shape[1] // CH
    for h in range(heads):
        cols = span_rows(h)
        first = dot_tn(key_ref[0:CH, cols], value_ref[0:CH, cols])
        second = dot_tn(key_ref[CH : 2 * CH, cols], value_ref[CH : 2 * CH, cols])
        first_ref[cols, :] = first.astype(BF16)
        put_slices(total_ref, first + second, h, total_ref.shape[1])


def span_states(key_rows, value_rows, shards):
    tokens, width = key_rows.shape
    return pl.pallas_call(
        state_kernel,
        out_shape=(shaped((shards, width // shards, CH), BF16), shaped((width, CH), BF16)),
        in_specs=[pl.BlockSpec(memory_space=pltpu.MemorySpace.HBM)] * 2,
        scratch_shapes=[
            pltpu.VMEM((tokens, width), BF16),
            pltpu.VMEM((tokens, width), BF16),
            pltpu.SemaphoreType.DMA((2,)),
        ],
        name="span_states",
        interpret=INTERPRET,
        compiler_params=pltpu.CompilerParams(vmem_limit_bytes=16 * 1024 * 1024),
    )(key_rows, value_rows)


def low_state_kernel(place_ref, one_ref, two_ref, three_ref, state_ref):
    row = place_ref[0] & ((1 << ROW_BITS) - 1)
    one = one_ref[...].astype(F32)
    two = two_ref[...].astype(F32)
    three = three_ref[...].astype(F32)
    state_ref[0] = jnp.where((row & 1) == 1, one, 0.0).astype(BF16)
    pair = jnp.where(row == 2, two + one, jnp.where(row == 3, three + two, 0.0))
    state_ref[1] = pair.astype(BF16)


def low_grad_kernel(one_ref, two_ref, three_ref, sum_ref):
    sum_ref[...] = one_ref[...].astype(F32) + two_ref[...].astype(F32) + three_ref[...].astype(F32)


def prefix_kernel(in_ref, out_ref):
    shards, height = in_ref.shape[0], in_ref.shape[1]
    levels = out_ref.shape[1] // height
    sums = [in_ref[s].astype(F32) for s in range(shards)]
    for _ in range(ROW_BITS):
        sums = [sums[2 * i] + sums[2 * i + 1] for i in range(len(sums) // 2)]
    zero = jnp.zeros(in_ref.shape[1:], BF16)
    for level in range(levels):
        rounded = [s.astype(BF16) for s in sums]
        for t in range(shards):
            group = t >> (level + ROW_BITS)
            out_ref[t, level * height : (level + 1) * height, :] = rounded[group - 1] if group & 1 else zero
        sums = [sums[2 * i] + sums[2 * i + 1] for i in range(len(sums) // 2)]


def suffix_kernel(in_ref, table_ref, out_ref):
    shards = in_ref.shape[0]
    levels = shards.bit_length() - 1 - ROW_BITS
    height = (in_ref.shape[1] - 8) // levels
    start = levels * height
    table_rows = table_ref.shape[0]
    rows = out_ref.shape[1] - height - table_rows
    gain = in_ref[0, start:, :].astype(F32)
    for s in range(1, shards):
        gain = gain + in_ref[s, start:, :].astype(F32)
    gain = (gain[:rows] + gain[rows : 2 * rows]).astype(BF16)
    tail = jnp.concatenate([table_ref[...], gain], axis=0)
    carried = [None]
    for level in range(levels - 1, -1, -1):
        size = 1 << (level + ROW_BITS)
        groups = shards >> (level + ROW_BITS)
        below = []
        for g in range(groups):
            base = carried[g >> 1]
            if g & 1 == 0:
                total = None
                for s in range((g + 1) * size, (g + 2) * size):
                    piece = in_ref[s, level * height : (level + 1) * height, :].astype(F32)
                    total = piece if total is None else total + piece
                base = total if base is None else base + total
            below.append(base)
        carried = below
    zero = jnp.zeros((height, CH), F32)
    for t in range(shards):
        value = zero if carried[t >> ROW_BITS] is None else carried[t >> ROW_BITS]
        out_ref[t, 0:height, :] = value.astype(BF16)
        out_ref[t, height:, :] = tail


def onehot_of(index_ref, level):
    tokens = index_ref.shape[1]
    entry = lax.broadcasted_iota(jnp.int32, (TABLE, tokens), 0)
    return (index_ref[level : level + 1, :] == entry).astype(F32)


def weight_kernel(index_ref, table_ref, weight_ref):
    levels, tokens = index_ref.shape
    heads = table_ref.shape[1]
    rows = [dot_nn(table_ref[level], onehot_of(index_ref, level), HIGHEST) for level in range(levels)]
    rows.append(jnp.zeros((CH - levels * heads, tokens), F32))
    weight_ref[...] = jnp.concatenate(rows, axis=0).T


def near_kernel(query_ref, key_ref, value_ref, first_ref, low_ref, weight_ref, out_ref):
    heads = query_ref.shape[1] // CH
    spans = query_ref.shape[0] // CH
    causal = causal_mask()
    for c in range(spans):
        rows = span_rows(c)
        for h in range(heads):
            cols = span_rows(h)
            query = query_ref[rows, cols]
            scores = jnp.where(causal, dot_nt(query, key_ref[rows, cols]), 0.0).astype(BF16)
            near = weight_ref[rows, h : h + 1] * dot_nn(scores, value_ref[rows, cols])
            if c == 1:
                near = near + weight_ref[rows, heads + h : heads + h + 1] * dot_nn(query, first_ref[cols, :])
            for level in range(ROW_BITS):
                spot = (level + 2) * heads + h
                near = near + weight_ref[rows, spot : spot + 1] * dot_nn(query, low_ref[level, cols, :])
            out_ref[rows, cols] = near


def far_kernel(near_ref, query_ref, state_ref, weight_ref, attn_ref):
    heads = query_ref.shape[1] // CH
    spans = query_ref.shape[0] // CH
    height = height_of(heads, state_ref)
    levels = state_ref.shape[1] // height
    for c in range(spans):
        rows = span_rows(c)
        for h in range(heads):
            cols = span_rows(h)
            query = query_ref[rows, cols]
            total = near_ref[rows, cols]
            for level in range(levels):
                spot = (level + 2 + ROW_BITS) * heads + h
                total = total + weight_ref[rows, spot : spot + 1] * dot_nn(query, get_slices(state_ref, h, height, level))
            attn_ref[rows, cols] = total.astype(BF16)


def norm_kernel(attn_ref, cot_ref, gain_ref, normed_ref, grad_ref):
    columns, own, width = attn_ref.shape
    features = float(columns * width)
    squares = jnp.zeros((own, width), F32)
    along = jnp.zeros((own, width), F32)
    for d in range(columns):
        cols = slice(d * width, (d + 1) * width)
        attn = attn_ref[d].astype(F32)
        squares = squares + attn * attn
        along = along + cot_ref[:, cols].astype(F32) * gain_ref[:, cols] * attn
    inv_rms = lax.rsqrt(jnp.sum(squares, axis=1, keepdims=True) / features + EPSILON)
    mean = jnp.sum(along, axis=1, keepdims=True) * inv_rms / features
    parts = []
    for d in range(columns):
        cols = slice(d * width, (d + 1) * width)
        cot = cot_ref[:, cols].astype(F32)
        unit = attn_ref[d].astype(F32) * inv_rms
        normed_ref[:, cols] = (unit * gain_ref[:, cols]).astype(BF16)
        grad_ref[d, 0:own, :] = ((cot * gain_ref[:, cols] - unit * mean) * inv_rms).astype(BF16)
        parts.append(jnp.sum(cot * unit, axis=0, keepdims=True))
    block = jnp.concatenate(parts, axis=0).astype(BF16)
    for d in range(columns):
        grad_ref[d, own:, :] = block


def grad_kernel(place_ref, head_ref, query_ref, weight_ref, grad_ref, group_ref, one_ref, two_ref):
    columns = head_ref.shape[0]
    own = head_ref.shape[1] - columns
    heads = query_ref.shape[1] // CH
    shards = group_ref.shape[0]
    height = height_of(heads, group_ref)
    levels = group_ref.shape[1] // height
    start = levels * height
    for d in range(columns):
        grad_ref[d * own : (d + 1) * own, :] = head_ref[d, 0:own, :]
    for h in range(heads):
        cols = span_rows(h)
        grad_f = grad_ref[:, cols].astype(F32)
        query = query_ref[:, cols]
        low = []
        for level in range(levels + ROW_BITS):
            spot = (level + 2) * heads + h
            product = dot_tn(query, (weight_ref[:, spot : spot + 1] * grad_f).astype(BF16))
            if level < ROW_BITS:
                low.append(product)
            else:
                put_slices(group_ref, product, h, height, level - ROW_BITS)
        one_ref[cols, :] = jnp.where((place_ref[0] & 1) == 1, low[0], low[1]).astype(BF16)
        two_ref[cols, :] = low[1].astype(BF16)
    gain = head_ref[0, own:, :].astype(F32)
    for d in range(1, columns):
        gain = gain + head_ref[d, own:, :].astype(F32)
    rows = columns * heads // shards
    extra = group_ref.shape[1] - start
    for s in range(shards):
        spots = range(s * rows, (s + 1) * rows)
        picked = [gain[i // heads : i // heads + 1, span_rows(i % heads)] for i in spots]
        high, low = split_pair(jnp.concatenate(picked, axis=0))
        fill = jnp.zeros((extra - 2 * rows, CH), BF16)
        group_ref[s, start:, :] = jnp.concatenate([high, low, fill], axis=0)


def back_kernel(
    query_ref, key_ref, value_ref, grad_ref, weight_ref, state_ref, low_ref, first_ref, index_ref,
    dq_ref, dk_ref, dv_ref, inner_ref, table_ref, gw_ref,
):
    heads = query_ref.shape[1] // CH
    spans = query_ref.shape[0] // CH
    height = height_of(heads, state_ref)
    levels = state_ref.shape[1] // height + ROW_BITS
    all_levels = levels + 2
    causal = causal_mask()
    gw_ref[...] = jnp.zeros(gw_ref.shape, F32)
    for c in range(spans):
        rows = span_rows(c)
        for h in range(heads):
            cols = span_rows(h)
            query = query_ref[rows, cols]
            query_f = query.astype(F32)
            key = key_ref[rows, cols]
            grad = grad_ref[rows, cols]
            first_weight = weight_ref[rows, h : h + 1]
            scores = jnp.where(causal, dot_nt(query, key), 0.0)
            along = jnp.where(causal, dot_nt(grad, value_ref[rows, cols]), 0.0)
            gw_ref[rows, h : h + 1] = jnp.sum(scores.astype(BF16).astype(F32) * along, axis=1, keepdims=True)
            grad_scores = (along * first_weight).astype(BF16)
            weighted = (scores * first_weight).astype(BF16)
            dq = dot_nn(grad_scores, key)
            dk_ref[rows, cols] = dot_tn(grad_scores, query)
            dv_ref[rows, cols] = dot_tn(weighted, grad)
            if c == 1:
                spot = heads + h
                weight = weight_ref[rows, spot : spot + 1]
                far = dot_nt(grad, first_ref[cols, :])
                gw_ref[rows, spot : spot + 1] = jnp.sum(query_f * far, axis=1, keepdims=True)
                dq = dq + weight * far
                inner_ref[cols, :] = dot_tn(query, (weight * grad.astype(F32)).astype(BF16))
            for level in range(levels):
                spot = (level + 2) * heads + h
                if level < ROW_BITS:
                    state = low_ref[level, cols, :]
                else:
                    state = get_slices(state_ref, h, height, level - ROW_BITS)
                far = dot_nt(grad, state)
                gw_ref[rows, spot : spot + 1] = jnp.sum(query_f * far, axis=1, keepdims=True)
                dq = dq + weight_ref[rows, spot : spot + 1] * far
            dq_ref[rows, cols] = dq.astype(BF16)
    grads = gw_ref[...].T
    blocks = []
    for level in range(all_levels):
        by_row = lax.dot_general(
            grads, onehot_of(index_ref, level), (((1,), (1,)), ((), ())), precision=HIGHEST, preferred_element_type=F32
        )
        blocks.append(by_row[level * heads : (level + 1) * heads])
    joined = [jnp.concatenate(blocks[2 * pair : 2 * pair + 2], axis=1) for pair in range(all_levels // 2)]
    for h in range(0, heads if all_levels % 2 else 0, 2):
        joined.append(jnp.concatenate([blocks[-1][h : h + 1], blocks[-1][h + 1 : h + 2]], axis=1))
    table_ref[...] = jnp.concatenate(joined, axis=0).astype(BF16)


def final_kernel(
    cross_ref, low_ref, inner_ref, key_ref, value_ref, dk_ref, dv_ref, grad_key_ref, grad_value_ref, table_ref, gain_ref
):
    heads = key_ref.shape[1] // CH
    spans = key_ref.shape[0] // CH
    shards = cross_ref.shape[0]
    height = height_of(heads, cross_ref)
    rows = gain_ref.shape[0] // shards
    table_end = cross_ref.shape[1] - height - rows
    total = None
    for s in range(shards):
        tail = cross_ref[s, height:, :].astype(F32)
        total = tail if total is None else total + tail
        gain_ref[s * rows : (s + 1) * rows, :] = tail[table_end:]
    all_levels = table_ref.shape[0]
    for level in range(all_levels):
        if level == all_levels - 1 and all_levels % 2:
            base = (level // 2) * heads
            for h in range(heads):
                spot, left = base + h // 2, (h % 2) * TABLE
                table_ref[level, h : h + 1, :] = total[spot : spot + 1, left : left + TABLE]
        else:
            top, left = (level // 2) * heads, (level % 2) * TABLE
            table_ref[level] = total[top : top + heads, left : left + TABLE]
    for h in range(heads):
        cols = span_rows(h)
        cross = get_slices(cross_ref, h, height).astype(F32) + low_ref[cols, :]
        for c in range(spans):
            rows = span_rows(c)
            state = (cross if c == 1 else inner_ref[cols, :] + cross).astype(BF16)
            grad_key = dk_ref[rows, cols] + dot_nt(value_ref[rows, cols], state)
            grad_value = dv_ref[rows, cols] + dot_nn(key_ref[rows, cols], state)
            grad_key_ref[rows, cols] = grad_key.astype(BF16)
            grad_value_ref[rows, cols] = grad_value.astype(BF16)


def exchange(value, axis):
    return lax.all_to_all(value, axis, split_axis=0, concat_axis=0, tiled=True)


def row_shift(value, step):
    row = 1 << ROW_BITS
    shards = lax.axis_size("seq")
    pairs = [(s, s + step) for s in range(shards) if 0 <= s % row + step < row]
    return lax.ppermute(value, "seq", pairs)


def body(queries, key_rows, value_rows, level_table, level_index, norm_gain, cotangent):
    tokens, width = queries.shape
    heads = level_table.shape[2]
    all_levels = level_table.shape[1]
    shards = lax.axis_size("seq")
    columns = lax.axis_size("head")
    levels = shards.bit_length() - 1 - ROW_BITS
    height = heads * CH // shards
    own = tokens // columns
    table_rows = all_levels * heads * TABLE // CH
    gain_rows = columns * heads // shards

    spot = lax.axis_index("seq").reshape(1)

    total, first = span_states(key_rows, value_rows, shards)
    slices = exchange(total, "seq")
    flat = total.reshape(width, CH)
    shifts = [row_shift(flat, step) for step in (1, 2, 3)]
    low = call(low_state_kernel, shaped((ROW_BITS, width, CH), BF16), spot, *shifts)
    gain = norm_gain.reshape(1, columns * width)
    table = jnp.transpose(level_table, (1, 2, 0))
    index = jnp.transpose(level_index)
    weights = call(weight_kernel, shaped((tokens, CH), F32), index, table)
    near = call(near_kernel, shaped((tokens, width), F32), queries, key_rows, value_rows, first, low, weights)
    group_states = call(prefix_kernel, shaped((shards, levels * height, CH), BF16), slices)
    states = exchange(group_states, "seq")
    attn = call(far_kernel, shaped((tokens, width), BF16), near, queries, states, weights)
    token_attn = exchange(attn.reshape(columns, own, width), "head")
    normed, token_grad = call(
        norm_kernel,
        (shaped((own, columns * width), BF16), shaped((columns, own + columns, width), BF16)),
        token_attn,
        cotangent,
        gain,
    )
    head_grad = exchange(token_grad, "head")
    grad, groups, low_one, low_two = call(
        grad_kernel,
        (
            shaped((tokens, width), BF16),
            shaped((shards, levels * height + 8, CH), BF16),
            shaped((width, CH), BF16),
            shaped((width, CH), BF16),
        ),
        spot,
        head_grad,
        queries,
        weights,
    )
    group_slices = exchange(groups, "seq")
    shifts = [row_shift(low_one if step == 1 else low_two, -step) for step in (1, 2, 3)]
    low_sum = call(low_grad_kernel, shaped((width, CH), F32), *shifts)
    grad_query, near_dk, near_dv, inner, table_part, _ = call(
        back_kernel,
        (
            shaped((tokens, width), BF16),
            shaped((tokens, width), F32),
            shaped((tokens, width), F32),
            shaped((heads * CH, CH), F32),
            shaped((table_rows, CH), BF16),
            shaped((tokens, CH), F32),
        ),
        queries,
        key_rows,
        value_rows,
        grad,
        weights,
        states,
        low,
        first,
        index,
    )
    key_slices = call(
        suffix_kernel, shaped((shards, height + table_rows + gain_rows, CH), BF16), group_slices, table_part
    )
    cross = exchange(key_slices, "seq")
    grad_key, grad_value, table_sum, gain_sum = call(
        final_kernel,
        (
            shaped((tokens, width), BF16),
            shaped((tokens, width), BF16),
            shaped((all_levels, heads, TABLE), F32),
            shaped((columns * heads, CH), F32),
        ),
        cross,
        low_sum,
        inner,
        key_rows,
        value_rows,
        near_dk,
        near_dv,
    )
    grad_table = jnp.transpose(table_sum, (2, 0, 1))
    return normed, grad_query, grad_key, grad_value, grad_table, gain_sum.reshape(columns * width)


def solution(mesh):
    placed = (
        P("seq", "head"),
        P("seq", "head"),
        P("seq", "head"),
        P(None, None, "head"),
        P("seq", None),
        P(),
        P(("seq", "head"), None),
    )
    return jax.shard_map(
        body,
        mesh=mesh,
        in_specs=placed,
        out_specs=(
            P(("seq", "head"), None),
            P("seq", "head"),
            P("seq", "head"),
            P("seq", "head"),
            P(None, None, "head"),
            P(),
        ),
        check_vma=False,
    )
```

```python
import jax
import jax.numpy as jnp
from jax import lax
from jax.experimental import pallas as pl
from jax.experimental.pallas import tpu as pltpu
from jax.sharding import PartitionSpec as P

CH = 128
TABLE = 64
EPSILON = 1e-06
HIGHEST = lax.Precision.HIGHEST
F32 = jnp.float32
BF16 = jnp.bfloat16
INTERPRET = False
ROW_BITS = 2


def in_hbm(value):
    return pltpu.with_memory_space_constraint(value, pltpu.MemorySpace.HBM)


def call(kernel, out_shape, *operands, hbm=(), hbm_out=(), scratch=()):
    whole = pl.BlockSpec(memory_space=pltpu.VMEM)
    scalar = pl.BlockSpec(memory_space=pltpu.SMEM)
    apart = pl.BlockSpec(memory_space=pltpu.MemorySpace.HBM)
    if isinstance(out_shape, tuple):
        out_specs = tuple(apart if i in hbm_out else whole for i in range(len(out_shape)))
    else:
        out_specs = whole
    return pl.pallas_call(
        kernel,
        out_shape=out_shape,
        in_specs=[
            apart if i in hbm else scalar if operand.ndim == 1 else whole for i, operand in enumerate(operands)
        ],
        out_specs=out_specs,
        scratch_shapes=scratch,
        interpret=INTERPRET,
        compiler_params=pltpu.CompilerParams(vmem_limit_bytes=16 * 1024 * 1024),
    )(*operands)


def shaped(shape, dtype):
    return jax.ShapeDtypeStruct(shape, dtype)


def dot_nn(a, b, precision=None):
    return lax.dot_general(a, b, (((1,), (0,)), ((), ())), precision=precision, preferred_element_type=F32)


def dot_nt(a, b):
    return lax.dot_general(a, b, (((1,), (1,)), ((), ())), preferred_element_type=F32)


def dot_tn(a, b, precision=None):
    return lax.dot_general(a, b, (((0,), (0,)), ((), ())), precision=precision, preferred_element_type=F32)


def causal_mask():
    rows = lax.broadcasted_iota(jnp.int32, (CH, CH), 0)
    cols = lax.broadcasted_iota(jnp.int32, (CH, CH), 1)
    return cols <= rows


def span_rows(c):
    return slice(c * CH, (c + 1) * CH)


def put_slices(ref, value, head, height, level=0):
    per_head = CH // height
    pieces = value.astype(BF16).reshape(per_head, height, value.shape[1])
    ref[head * per_head : (head + 1) * per_head, level * height : (level + 1) * height, :] = pieces


def get_slices(ref, head, height, level=0):
    per_head = CH // height
    pieces = ref[head * per_head : (head + 1) * per_head, level * height : (level + 1) * height, :]
    return pieces.reshape(CH, ref.shape[2])


def height_of(heads, ref):
    return heads * CH // ref.shape[0]


def split_pair(value):
    high = value.astype(BF16)
    return high, (value - high.astype(F32)).astype(BF16)


def state_kernel(key_hbm, value_hbm, total_ref, first_ref, key_ref, value_ref, sems):
    key_copy = pltpu.make_async_copy(key_hbm, key_ref, sems.at[0])
    value_copy = pltpu.make_async_copy(value_hbm, value_ref, sems.at[1])
    key_copy.start()
    value_copy.start()
    key_copy.wait()
    value_copy.wait()
    heads = key_ref.shape[1] // CH
    for h in range(heads):
        cols = span_rows(h)
        first = dot_tn(key_ref[0:CH, cols], value_ref[0:CH, cols])
        second = dot_tn(key_ref[CH : 2 * CH, cols], value_ref[CH : 2 * CH, cols])
        first_ref[cols, :] = first.astype(BF16)
        put_slices(total_ref, first + second, h, total_ref.shape[1])


def span_states(key_rows, value_rows, shards):
    tokens, width = key_rows.shape
    return pl.pallas_call(
        state_kernel,
        out_shape=(shaped((shards, width // shards, CH), BF16), shaped((width, CH), BF16)),
        in_specs=[pl.BlockSpec(memory_space=pltpu.MemorySpace.HBM)] * 2,
        scratch_shapes=[
            pltpu.VMEM((tokens, width), BF16),
            pltpu.VMEM((tokens, width), BF16),
            pltpu.SemaphoreType.DMA((2,)),
        ],
        name="span_states",
        interpret=INTERPRET,
        compiler_params=pltpu.CompilerParams(vmem_limit_bytes=16 * 1024 * 1024),
    )(in_hbm(key_rows), in_hbm(value_rows))


def low_state_kernel(place_ref, one_ref, two_ref, three_ref, state_ref):
    row = place_ref[0] & ((1 << ROW_BITS) - 1)
    one = one_ref[...].astype(F32)
    two = two_ref[...].astype(F32)
    three = three_ref[...].astype(F32)
    state_ref[0] = jnp.where((row & 1) == 1, one, 0.0).astype(BF16)
    pair = jnp.where(row == 2, two + one, jnp.where(row == 3, three + two, 0.0))
    state_ref[1] = pair.astype(BF16)


def low_grad_kernel(one_ref, two_ref, three_ref, sum_ref):
    sum_ref[...] = one_ref[...].astype(F32) + two_ref[...].astype(F32) + three_ref[...].astype(F32)


def prefix_kernel(in_ref, out_ref):
    shards, height = in_ref.shape[0], in_ref.shape[1]
    levels = out_ref.shape[1] // height
    sums = [in_ref[s].astype(F32) for s in range(shards)]
    for _ in range(ROW_BITS):
        sums = [sums[2 * i] + sums[2 * i + 1] for i in range(len(sums) // 2)]
    zero = jnp.zeros(in_ref.shape[1:], BF16)
    for level in range(levels):
        rounded = [s.astype(BF16) for s in sums]
        for t in range(shards):
            group = t >> (level + ROW_BITS)
            out_ref[t, level * height : (level + 1) * height, :] = rounded[group - 1] if group & 1 else zero
        sums = [sums[2 * i] + sums[2 * i + 1] for i in range(len(sums) // 2)]


def suffix_kernel(in_ref, table_ref, out_ref):
    shards = in_ref.shape[0]
    levels = shards.bit_length() - 1 - ROW_BITS
    height = (in_ref.shape[1] - 8) // levels
    start = levels * height
    table_rows = table_ref.shape[0]
    rows = out_ref.shape[1] - height - table_rows
    gain = in_ref[0, start:, :].astype(F32)
    for s in range(1, shards):
        gain = gain + in_ref[s, start:, :].astype(F32)
    gain = (gain[:rows] + gain[rows : 2 * rows]).astype(BF16)
    tail = jnp.concatenate([table_ref[...], gain], axis=0)
    carried = [None]
    for level in range(levels - 1, -1, -1):
        size = 1 << (level + ROW_BITS)
        groups = shards >> (level + ROW_BITS)
        below = []
        for g in range(groups):
            base = carried[g >> 1]
            if g & 1 == 0:
                total = None
                for s in range((g + 1) * size, (g + 2) * size):
                    piece = in_ref[s, level * height : (level + 1) * height, :].astype(F32)
                    total = piece if total is None else total + piece
                base = total if base is None else base + total
            below.append(base)
        carried = below
    zero = jnp.zeros((height, CH), F32)
    for t in range(shards):
        value = zero if carried[t >> ROW_BITS] is None else carried[t >> ROW_BITS]
        out_ref[t, 0:height, :] = value.astype(BF16)
        out_ref[t, height:, :] = tail


def onehot_of(index_ref, level):
    tokens = index_ref.shape[1]
    entry = lax.broadcasted_iota(jnp.int32, (TABLE, tokens), 0)
    return (index_ref[level : level + 1, :] == entry).astype(F32)


def weight_kernel(index_ref, table_ref, weight_ref):
    levels, tokens = index_ref.shape
    heads = table_ref.shape[1]
    rows = [dot_nn(table_ref[level], onehot_of(index_ref, level), HIGHEST) for level in range(levels)]
    rows.append(jnp.zeros((CH - levels * heads, tokens), F32))
    weight_ref[...] = jnp.concatenate(rows, axis=0).T


def near_kernel(query_ref, key_ref, value_ref, first_ref, low_ref, weight_ref, out_ref):
    heads = query_ref.shape[1] // CH
    spans = query_ref.shape[0] // CH
    causal = causal_mask()
    for c in range(spans):
        rows = span_rows(c)
        for h in range(heads):
            cols = span_rows(h)
            query = query_ref[rows, cols]
            scores = jnp.where(causal, dot_nt(query, key_ref[rows, cols]), 0.0).astype(BF16)
            near = weight_ref[rows, h : h + 1] * dot_nn(scores, value_ref[rows, cols])
            if c == 1:
                near = near + weight_ref[rows, heads + h : heads + h + 1] * dot_nn(query, first_ref[cols, :])
            for level in range(ROW_BITS):
                spot = (level + 2) * heads + h
                near = near + weight_ref[rows, spot : spot + 1] * dot_nn(query, low_ref[level, cols, :])
            out_ref[rows, cols] = near


def far_kernel(near_ref, query_ref, state_ref, weight_ref, attn_ref):
    heads = query_ref.shape[1] // CH
    spans = query_ref.shape[0] // CH
    height = height_of(heads, state_ref)
    levels = state_ref.shape[1] // height
    for c in range(spans):
        rows = span_rows(c)
        for h in range(heads):
            cols = span_rows(h)
            query = query_ref[rows, cols]
            total = near_ref[rows, cols]
            for level in range(levels):
                spot = (level + 2 + ROW_BITS) * heads + h
                total = total + weight_ref[rows, spot : spot + 1] * dot_nn(query, get_slices(state_ref, h, height, level))
            attn_ref[rows, cols] = total.astype(BF16)


def norm_kernel(attn_ref, cot_ref, gain_ref, normed_ref, grad_ref):
    columns, own, width = attn_ref.shape
    features = float(columns * width)
    squares = jnp.zeros((own, width), F32)
    along = jnp.zeros((own, width), F32)
    for d in range(columns):
        cols = slice(d * width, (d + 1) * width)
        attn = attn_ref[d].astype(F32)
        squares = squares + attn * attn
        along = along + cot_ref[:, cols].astype(F32) * gain_ref[:, cols] * attn
    inv_rms = lax.rsqrt(jnp.sum(squares, axis=1, keepdims=True) / features + EPSILON)
    mean = jnp.sum(along, axis=1, keepdims=True) * inv_rms / features
    parts = []
    for d in range(columns):
        cols = slice(d * width, (d + 1) * width)
        cot = cot_ref[:, cols].astype(F32)
        unit = attn_ref[d].astype(F32) * inv_rms
        normed_ref[:, cols] = (unit * gain_ref[:, cols]).astype(BF16)
        grad_ref[d, 0:own, :] = ((cot * gain_ref[:, cols] - unit * mean) * inv_rms).astype(BF16)
        parts.append(jnp.sum(cot * unit, axis=0, keepdims=True))
    block = jnp.concatenate(parts, axis=0).astype(BF16)
    for d in range(columns):
        grad_ref[d, own:, :] = block


def grad_kernel(place_ref, head_ref, query_ref, weight_ref, grad_hbm, group_ref, one_ref, two_ref, grad_ref, sem):
    columns = head_ref.shape[0]
    own = head_ref.shape[1] - columns
    heads = query_ref.shape[1] // CH
    shards = group_ref.shape[0]
    height = height_of(heads, group_ref)
    levels = group_ref.shape[1] // height
    start = levels * height
    for d in range(columns):
        grad_ref[d * own : (d + 1) * own, :] = head_ref[d, 0:own, :]
    grad_copy = pltpu.make_async_copy(grad_ref, grad_hbm, sem)
    grad_copy.start()
    for h in range(heads):
        cols = span_rows(h)
        grad_f = grad_ref[:, cols].astype(F32)
        query = query_ref[:, cols]
        low = []
        for level in range(levels + ROW_BITS):
            spot = (level + 2) * heads + h
            product = dot_tn(query, (weight_ref[:, spot : spot + 1] * grad_f).astype(BF16))
            if level < ROW_BITS:
                low.append(product)
            else:
                put_slices(group_ref, product, h, height, level - ROW_BITS)
        one_ref[cols, :] = jnp.where((place_ref[0] & 1) == 1, low[0], low[1]).astype(BF16)
        two_ref[cols, :] = low[1].astype(BF16)
    gain = head_ref[0, own:, :].astype(F32)
    for d in range(1, columns):
        gain = gain + head_ref[d, own:, :].astype(F32)
    rows = columns * heads // shards
    extra = group_ref.shape[1] - start
    for s in range(shards):
        spots = range(s * rows, (s + 1) * rows)
        picked = [gain[i // heads : i // heads + 1, span_rows(i % heads)] for i in spots]
        high, low = split_pair(jnp.concatenate(picked, axis=0))
        fill = jnp.zeros((extra - 2 * rows, CH), BF16)
        group_ref[s, start:, :] = jnp.concatenate([high, low, fill], axis=0)
    grad_copy.wait()


def back_kernel(
    query_ref, key_ref, value_ref, grad_hbm, weight_ref, state_ref, low_ref, first_ref, index_ref,
    dq_ref, dk_ref, dv_ref, inner_ref, table_ref, gw_ref, grad_ref, sem,
):
    grad_copy = pltpu.make_async_copy(grad_hbm, grad_ref, sem)
    grad_copy.start()
    grad_copy.wait()
    heads = query_ref.shape[1] // CH
    spans = query_ref.shape[0] // CH
    height = height_of(heads, state_ref)
    levels = state_ref.shape[1] // height + ROW_BITS
    all_levels = levels + 2
    causal = causal_mask()
    gw_ref[...] = jnp.zeros(gw_ref.shape, F32)
    for c in range(spans):
        rows = span_rows(c)
        for h in range(heads):
            cols = span_rows(h)
            query = query_ref[rows, cols]
            query_f = query.astype(F32)
            key = key_ref[rows, cols]
            grad = grad_ref[rows, cols]
            first_weight = weight_ref[rows, h : h + 1]
            scores = jnp.where(causal, dot_nt(query, key), 0.0)
            along = jnp.where(causal, dot_nt(grad, value_ref[rows, cols]), 0.0)
            gw_ref[rows, h : h + 1] = jnp.sum(scores.astype(BF16).astype(F32) * along, axis=1, keepdims=True)
            grad_scores = (along * first_weight).astype(BF16)
            weighted = (scores * first_weight).astype(BF16)
            dq = dot_nn(grad_scores, key)
            dk_ref[rows, cols] = dot_tn(grad_scores, query)
            dv_ref[rows, cols] = dot_tn(weighted, grad)
            if c == 1:
                spot = heads + h
                weight = weight_ref[rows, spot : spot + 1]
                far = dot_nt(grad, first_ref[cols, :])
                gw_ref[rows, spot : spot + 1] = jnp.sum(query_f * far, axis=1, keepdims=True)
                dq = dq + weight * far
                inner_ref[cols, :] = dot_tn(query, (weight * grad.astype(F32)).astype(BF16))
            for level in range(levels):
                spot = (level + 2) * heads + h
                if level < ROW_BITS:
                    state = low_ref[level, cols, :]
                else:
                    state = get_slices(state_ref, h, height, level - ROW_BITS)
                far = dot_nt(grad, state)
                gw_ref[rows, spot : spot + 1] = jnp.sum(query_f * far, axis=1, keepdims=True)
                dq = dq + weight_ref[rows, spot : spot + 1] * far
            dq_ref[rows, cols] = dq.astype(BF16)
    grads = gw_ref[...].T
    blocks = []
    for level in range(all_levels):
        by_row = lax.dot_general(
            grads, onehot_of(index_ref, level), (((1,), (1,)), ((), ())), precision=HIGHEST, preferred_element_type=F32
        )
        blocks.append(by_row[level * heads : (level + 1) * heads])
    joined = [jnp.concatenate(blocks[2 * pair : 2 * pair + 2], axis=1) for pair in range(all_levels // 2)]
    for h in range(0, heads if all_levels % 2 else 0, 2):
        joined.append(jnp.concatenate([blocks[-1][h : h + 1], blocks[-1][h + 1 : h + 2]], axis=1))
    table_ref[...] = jnp.concatenate(joined, axis=0).astype(BF16)


def final_kernel(
    cross_ref, low_ref, inner_ref, key_ref, value_ref, dk_ref, dv_ref, grad_key_ref, grad_value_ref, table_ref, gain_ref
):
    heads = key_ref.shape[1] // CH
    spans = key_ref.shape[0] // CH
    shards = cross_ref.shape[0]
    height = height_of(heads, cross_ref)
    rows = gain_ref.shape[0] // shards
    table_end = cross_ref.shape[1] - height - rows
    total = None
    for s in range(shards):
        tail = cross_ref[s, height:, :].astype(F32)
        total = tail if total is None else total + tail
        gain_ref[s * rows : (s + 1) * rows, :] = tail[table_end:]
    all_levels = table_ref.shape[0]
    for level in range(all_levels):
        if level == all_levels - 1 and all_levels % 2:
            base = (level // 2) * heads
            for h in range(heads):
                spot, left = base + h // 2, (h % 2) * TABLE
                table_ref[level, h : h + 1, :] = total[spot : spot + 1, left : left + TABLE]
        else:
            top, left = (level // 2) * heads, (level % 2) * TABLE
            table_ref[level] = total[top : top + heads, left : left + TABLE]
    for h in range(heads):
        cols = span_rows(h)
        cross = get_slices(cross_ref, h, height).astype(F32) + low_ref[cols, :]
        for c in range(spans):
            rows = span_rows(c)
            state = (cross if c == 1 else inner_ref[cols, :] + cross).astype(BF16)
            grad_key = dk_ref[rows, cols] + dot_nt(value_ref[rows, cols], state)
            grad_value = dv_ref[rows, cols] + dot_nn(key_ref[rows, cols], state)
            grad_key_ref[rows, cols] = grad_key.astype(BF16)
            grad_value_ref[rows, cols] = grad_value.astype(BF16)


def exchange(value, axis):
    return lax.all_to_all(value, axis, split_axis=0, concat_axis=0, tiled=True)


def row_shift(value, step):
    row = 1 << ROW_BITS
    shards = lax.axis_size("seq")
    pairs = [(s, s + step) for s in range(shards) if 0 <= s % row + step < row]
    return lax.ppermute(value, "seq", pairs)


def body(queries, key_rows, value_rows, level_table, level_index, norm_gain, cotangent):
    tokens, width = queries.shape
    heads = level_table.shape[2]
    all_levels = level_table.shape[1]
    shards = lax.axis_size("seq")
    columns = lax.axis_size("head")
    levels = shards.bit_length() - 1 - ROW_BITS
    height = heads * CH // shards
    own = tokens // columns
    table_rows = all_levels * heads * TABLE // CH
    gain_rows = columns * heads // shards

    spot = lax.axis_index("seq").reshape(1)

    total, first = span_states(key_rows, value_rows, shards)
    slices = exchange(total, "seq")
    flat = total.reshape(width, CH)
    shifts = [row_shift(flat, step) for step in (1, 2, 3)]
    low = call(low_state_kernel, shaped((ROW_BITS, width, CH), BF16), spot, *shifts)
    gain = norm_gain.reshape(1, columns * width)
    table = jnp.transpose(level_table, (1, 2, 0))
    index = jnp.transpose(level_index)
    weights = call(weight_kernel, shaped((tokens, CH), F32), index, table)
    near = call(near_kernel, shaped((tokens, width), F32), queries, key_rows, value_rows, first, low, weights)
    group_states = call(prefix_kernel, shaped((shards, levels * height, CH), BF16), slices)
    states = exchange(group_states, "seq")
    attn = call(far_kernel, shaped((tokens, width), BF16), near, queries, states, weights)
    token_attn = exchange(attn.reshape(columns, own, width), "head")
    normed, token_grad = call(
        norm_kernel,
        (shaped((own, columns * width), BF16), shaped((columns, own + columns, width), BF16)),
        token_attn,
        cotangent,
        gain,
    )
    head_grad = exchange(token_grad, "head")
    grad, groups, low_one, low_two = call(
        grad_kernel,
        (
            pltpu.MemorySpace.HBM((tokens, width), BF16),
            shaped((shards, levels * height + 8, CH), BF16),
            shaped((width, CH), BF16),
            shaped((width, CH), BF16),
        ),
        spot,
        head_grad,
        queries,
        weights,
        hbm_out=(0,),
        scratch=(pltpu.VMEM((tokens, width), BF16), pltpu.SemaphoreType.DMA),
    )
    group_slices = exchange(groups, "seq")
    shifts = [row_shift(low_one if step == 1 else low_two, -step) for step in (1, 2, 3)]
    low_sum = call(low_grad_kernel, shaped((width, CH), F32), *shifts)
    grad_query, near_dk, near_dv, inner, table_part = call(
        back_kernel,
        (
            shaped((tokens, width), BF16),
            shaped((tokens, width), F32),
            shaped((tokens, width), F32),
            shaped((heads * CH, CH), F32),
            shaped((table_rows, CH), BF16),
        ),
        queries,
        key_rows,
        value_rows,
        in_hbm(grad),
        weights,
        states,
        low,
        first,
        index,
        hbm=(3,),
        scratch=(pltpu.VMEM((tokens, CH), F32), pltpu.VMEM((tokens, width), BF16), pltpu.SemaphoreType.DMA),
    )
    key_slices = call(
        suffix_kernel, shaped((shards, height + table_rows + gain_rows, CH), BF16), group_slices, table_part
    )
    cross = exchange(key_slices, "seq")
    grad_key, grad_value, table_sum, gain_sum = call(
        final_kernel,
        (
            shaped((tokens, width), BF16),
            shaped((tokens, width), BF16),
            shaped((all_levels, heads, TABLE), F32),
            shaped((columns * heads, CH), F32),
        ),
        cross,
        low_sum,
        inner,
        key_rows,
        value_rows,
        near_dk,
        near_dv,
    )
    grad_table = jnp.transpose(table_sum, (2, 0, 1))
    return normed, grad_query, grad_key, grad_value, grad_table, gain_sum.reshape(columns * width)


def solution(mesh):
    placed = (
        P("seq", "head"),
        P("seq", "head"),
        P("seq", "head"),
        P(None, None, "head"),
        P("seq", None),
        P(),
        P(("seq", "head"), None),
    )
    return jax.shard_map(
        body,
        mesh=mesh,
        in_specs=placed,
        out_specs=(
            P(("seq", "head"), None),
            P("seq", "head"),
            P("seq", "head"),
            P("seq", "head"),
            P(None, None, "head"),
            P(),
        ),
        check_vma=False,
    )
```

```python
import jax
import jax.numpy as jnp
from jax import lax
from jax.experimental import pallas as pl
from jax.experimental.pallas import tpu as pltpu
from jax.sharding import PartitionSpec as P

CH = 128
TABLE = 64
EPSILON = 1e-06
HIGHEST = lax.Precision.HIGHEST
F32 = jnp.float32
BF16 = jnp.bfloat16
INTERPRET = False
ROW_BITS = 2


def in_hbm(value):
    return pltpu.with_memory_space_constraint(value, pltpu.MemorySpace.HBM)


def call(kernel, out_shape, *operands, hbm=(), hbm_out=(), scratch=()):
    whole = pl.BlockSpec(memory_space=pltpu.VMEM)
    scalar = pl.BlockSpec(memory_space=pltpu.SMEM)
    apart = pl.BlockSpec(memory_space=pltpu.MemorySpace.HBM)
    if isinstance(out_shape, tuple):
        out_specs = tuple(apart if i in hbm_out else whole for i in range(len(out_shape)))
    else:
        out_specs = whole
    return pl.pallas_call(
        kernel,
        out_shape=out_shape,
        in_specs=[
            apart if i in hbm else scalar if operand.ndim == 1 else whole for i, operand in enumerate(operands)
        ],
        out_specs=out_specs,
        scratch_shapes=scratch,
        interpret=INTERPRET,
        compiler_params=pltpu.CompilerParams(vmem_limit_bytes=16 * 1024 * 1024),
    )(*operands)


def shaped(shape, dtype):
    return jax.ShapeDtypeStruct(shape, dtype)


def dot_nn(a, b, precision=None):
    return lax.dot_general(a, b, (((1,), (0,)), ((), ())), precision=precision, preferred_element_type=F32)


def dot_nt(a, b):
    return lax.dot_general(a, b, (((1,), (1,)), ((), ())), preferred_element_type=F32)


def dot_tn(a, b, precision=None):
    return lax.dot_general(a, b, (((0,), (0,)), ((), ())), precision=precision, preferred_element_type=F32)


def causal_mask():
    rows = lax.broadcasted_iota(jnp.int32, (CH, CH), 0)
    cols = lax.broadcasted_iota(jnp.int32, (CH, CH), 1)
    return cols <= rows


def span_rows(c):
    return slice(c * CH, (c + 1) * CH)


def put_slices(ref, value, head, height, level=0):
    per_head = CH // height
    pieces = value.astype(BF16).reshape(per_head, height, value.shape[1])
    ref[head * per_head : (head + 1) * per_head, level * height : (level + 1) * height, :] = pieces


def get_slices(ref, head, height, level=0):
    per_head = CH // height
    pieces = ref[head * per_head : (head + 1) * per_head, level * height : (level + 1) * height, :]
    return pieces.reshape(CH, ref.shape[2])


def height_of(heads, ref):
    return heads * CH // ref.shape[0]


def split_pair(value):
    high = value.astype(BF16)
    return high, (value - high.astype(F32)).astype(BF16)


def state_kernel(key_hbm, value_hbm, total_ref, first_ref, key_ref, value_ref, sems):
    key_copy = pltpu.make_async_copy(key_hbm, key_ref, sems.at[0])
    value_copy = pltpu.make_async_copy(value_hbm, value_ref, sems.at[1])
    key_copy.start()
    value_copy.start()
    key_copy.wait()
    value_copy.wait()
    heads = key_ref.shape[1] // CH
    for h in range(heads):
        cols = span_rows(h)
        first = dot_tn(key_ref[0:CH, cols], value_ref[0:CH, cols])
        second = dot_tn(key_ref[CH : 2 * CH, cols], value_ref[CH : 2 * CH, cols])
        first_ref[cols, :] = first.astype(BF16)
        put_slices(total_ref, first + second, h, total_ref.shape[1])


def span_states(key_rows, value_rows, shards):
    tokens, width = key_rows.shape
    return pl.pallas_call(
        state_kernel,
        out_shape=(shaped((shards, width // shards, CH), BF16), shaped((width, CH), BF16)),
        in_specs=[pl.BlockSpec(memory_space=pltpu.MemorySpace.HBM)] * 2,
        scratch_shapes=[
            pltpu.VMEM((tokens, width), BF16),
            pltpu.VMEM((tokens, width), BF16),
            pltpu.SemaphoreType.DMA((2,)),
        ],
        name="span_states",
        interpret=INTERPRET,
        compiler_params=pltpu.CompilerParams(vmem_limit_bytes=16 * 1024 * 1024),
    )(in_hbm(key_rows), in_hbm(value_rows))


def low_state_kernel(place_ref, one_ref, two_ref, three_ref, state_ref):
    row = place_ref[0]
    pair = two_ref[...].astype(F32) + three_ref[...].astype(F32)
    state_ref[0] = jnp.where((row & 1) == 1, one_ref[...].astype(F32), 0.0).astype(BF16)
    state_ref[1] = jnp.where((row & 2) == 2, pair, 0.0).astype(BF16)


def low_grad_kernel(place_ref, one_ref, two_ref, three_ref, sum_ref):
    row = place_ref[0]
    pair = two_ref[...].astype(F32) + three_ref[...].astype(F32)
    total = jnp.where((row & 1) == 0, one_ref[...].astype(F32), 0.0)
    sum_ref[...] = total + jnp.where((row & 2) == 0, pair, 0.0)


def prefix_kernel(in_ref, out_ref):
    shards, height = in_ref.shape[0], in_ref.shape[1]
    levels = out_ref.shape[1] // height
    sums = [in_ref[s].astype(F32) for s in range(shards)]
    for _ in range(ROW_BITS):
        sums = [sums[2 * i] + sums[2 * i + 1] for i in range(len(sums) // 2)]
    zero = jnp.zeros(in_ref.shape[1:], BF16)
    for level in range(levels):
        rounded = [s.astype(BF16) for s in sums]
        for t in range(shards):
            group = t >> (level + ROW_BITS)
            out_ref[t, level * height : (level + 1) * height, :] = rounded[group - 1] if group & 1 else zero
        sums = [sums[2 * i] + sums[2 * i + 1] for i in range(len(sums) // 2)]


def suffix_kernel(in_ref, table_ref, out_ref):
    shards = in_ref.shape[0]
    levels = shards.bit_length() - 1 - ROW_BITS
    height = (in_ref.shape[1] - 8) // levels
    start = levels * height
    table_rows = table_ref.shape[0]
    rows = out_ref.shape[1] - height - table_rows
    gain = in_ref[0, start:, :].astype(F32)
    for s in range(1, shards):
        gain = gain + in_ref[s, start:, :].astype(F32)
    gain = (gain[:rows] + gain[rows : 2 * rows]).astype(BF16)
    tail = jnp.concatenate([table_ref[...], gain], axis=0)
    carried = [None]
    for level in range(levels - 1, -1, -1):
        size = 1 << (level + ROW_BITS)
        groups = shards >> (level + ROW_BITS)
        below = []
        for g in range(groups):
            base = carried[g >> 1]
            if g & 1 == 0:
                total = None
                for s in range((g + 1) * size, (g + 2) * size):
                    piece = in_ref[s, level * height : (level + 1) * height, :].astype(F32)
                    total = piece if total is None else total + piece
                base = total if base is None else base + total
            below.append(base)
        carried = below
    zero = jnp.zeros((height, CH), F32)
    for t in range(shards):
        value = zero if carried[t >> ROW_BITS] is None else carried[t >> ROW_BITS]
        out_ref[t, 0:height, :] = value.astype(BF16)
        out_ref[t, height:, :] = tail


def onehot_of(index_ref, level):
    tokens = index_ref.shape[1]
    entry = lax.broadcasted_iota(jnp.int32, (TABLE, tokens), 0)
    return (index_ref[level : level + 1, :] == entry).astype(F32)


def weight_kernel(index_ref, table_ref, weight_ref):
    levels, tokens = index_ref.shape
    heads = table_ref.shape[1]
    rows = [dot_nn(table_ref[level], onehot_of(index_ref, level), HIGHEST) for level in range(levels)]
    rows.append(jnp.zeros((CH - levels * heads, tokens), F32))
    weight_ref[...] = jnp.concatenate(rows, axis=0).T


def near_kernel(query_ref, key_ref, value_ref, first_ref, low_ref, weight_ref, out_ref):
    heads = query_ref.shape[1] // CH
    spans = query_ref.shape[0] // CH
    causal = causal_mask()
    for c in range(spans):
        rows = span_rows(c)
        for h in range(heads):
            cols = span_rows(h)
            query = query_ref[rows, cols]
            scores = jnp.where(causal, dot_nt(query, key_ref[rows, cols]), 0.0).astype(BF16)
            near = weight_ref[rows, h : h + 1] * dot_nn(scores, value_ref[rows, cols])
            if c == 1:
                near = near + weight_ref[rows, heads + h : heads + h + 1] * dot_nn(query, first_ref[cols, :])
            for level in range(ROW_BITS):
                spot = (level + 2) * heads + h
                near = near + weight_ref[rows, spot : spot + 1] * dot_nn(query, low_ref[level, cols, :])
            out_ref[rows, cols] = near


def far_kernel(near_ref, query_ref, state_ref, weight_ref, attn_ref):
    heads = query_ref.shape[1] // CH
    spans = query_ref.shape[0] // CH
    height = height_of(heads, state_ref)
    levels = state_ref.shape[1] // height
    for c in range(spans):
        rows = span_rows(c)
        for h in range(heads):
            cols = span_rows(h)
            query = query_ref[rows, cols]
            total = near_ref[rows, cols]
            for level in range(levels):
                spot = (level + 2 + ROW_BITS) * heads + h
                total = total + weight_ref[rows, spot : spot + 1] * dot_nn(query, get_slices(state_ref, h, height, level))
            attn_ref[rows, cols] = total.astype(BF16)


def norm_kernel(attn_ref, cot_ref, gain_ref, normed_ref, grad_ref):
    columns, own, width = attn_ref.shape
    features = float(columns * width)
    squares = jnp.zeros((own, width), F32)
    along = jnp.zeros((own, width), F32)
    for d in range(columns):
        cols = slice(d * width, (d + 1) * width)
        attn = attn_ref[d].astype(F32)
        squares = squares + attn * attn
        along = along + cot_ref[:, cols].astype(F32) * gain_ref[:, cols] * attn
    inv_rms = lax.rsqrt(jnp.sum(squares, axis=1, keepdims=True) / features + EPSILON)
    mean = jnp.sum(along, axis=1, keepdims=True) * inv_rms / features
    parts = []
    for d in range(columns):
        cols = slice(d * width, (d + 1) * width)
        cot = cot_ref[:, cols].astype(F32)
        unit = attn_ref[d].astype(F32) * inv_rms
        normed_ref[:, cols] = (unit * gain_ref[:, cols]).astype(BF16)
        grad_ref[d, 0:own, :] = ((cot * gain_ref[:, cols] - unit * mean) * inv_rms).astype(BF16)
        parts.append(jnp.sum(cot * unit, axis=0, keepdims=True))
    block = jnp.concatenate(parts, axis=0).astype(BF16)
    for d in range(columns):
        grad_ref[d, own:, :] = block


def grad_kernel(head_ref, query_ref, weight_ref, grad_hbm, group_ref, one_ref, two_ref, grad_ref, sem):
    columns = head_ref.shape[0]
    own = head_ref.shape[1] - columns
    heads = query_ref.shape[1] // CH
    shards = group_ref.shape[0]
    height = height_of(heads, group_ref)
    levels = group_ref.shape[1] // height
    start = levels * height
    for d in range(columns):
        grad_ref[d * own : (d + 1) * own, :] = head_ref[d, 0:own, :]
    grad_copy = pltpu.make_async_copy(grad_ref, grad_hbm, sem)
    grad_copy.start()
    for h in range(heads):
        cols = span_rows(h)
        grad_f = grad_ref[:, cols].astype(F32)
        query = query_ref[:, cols]
        low = []
        for level in range(levels + ROW_BITS):
            spot = (level + 2) * heads + h
            product = dot_tn(query, (weight_ref[:, spot : spot + 1] * grad_f).astype(BF16))
            if level < ROW_BITS:
                low.append(product)
            else:
                put_slices(group_ref, product, h, height, level - ROW_BITS)
        one_ref[cols, :] = low[0].astype(BF16)
        two_ref[cols, :] = low[1].astype(BF16)
    gain = head_ref[0, own:, :].astype(F32)
    for d in range(1, columns):
        gain = gain + head_ref[d, own:, :].astype(F32)
    rows = columns * heads // shards
    extra = group_ref.shape[1] - start
    for s in range(shards):
        spots = range(s * rows, (s + 1) * rows)
        picked = [gain[i // heads : i // heads + 1, span_rows(i % heads)] for i in spots]
        high, low = split_pair(jnp.concatenate(picked, axis=0))
        fill = jnp.zeros((extra - 2 * rows, CH), BF16)
        group_ref[s, start:, :] = jnp.concatenate([high, low, fill], axis=0)
    grad_copy.wait()


def back_kernel(
    query_ref, key_ref, value_ref, grad_hbm, weight_ref, state_ref, low_ref, first_ref, index_ref,
    dq_ref, dk_ref, dv_ref, inner_ref, table_ref, gw_ref, grad_ref, sem,
):
    grad_copy = pltpu.make_async_copy(grad_hbm, grad_ref, sem)
    grad_copy.start()
    grad_copy.wait()
    heads = query_ref.shape[1] // CH
    spans = query_ref.shape[0] // CH
    height = height_of(heads, state_ref)
    levels = state_ref.shape[1] // height + ROW_BITS
    all_levels = levels + 2
    causal = causal_mask()
    gw_ref[...] = jnp.zeros(gw_ref.shape, F32)
    for c in range(spans):
        rows = span_rows(c)
        for h in range(heads):
            cols = span_rows(h)
            query = query_ref[rows, cols]
            query_f = query.astype(F32)
            key = key_ref[rows, cols]
            grad = grad_ref[rows, cols]
            first_weight = weight_ref[rows, h : h + 1]
            scores = jnp.where(causal, dot_nt(query, key), 0.0)
            along = jnp.where(causal, dot_nt(grad, value_ref[rows, cols]), 0.0)
            gw_ref[rows, h : h + 1] = jnp.sum(scores.astype(BF16).astype(F32) * along, axis=1, keepdims=True)
            grad_scores = (along * first_weight).astype(BF16)
            weighted = (scores * first_weight).astype(BF16)
            dq = dot_nn(grad_scores, key)
            dk_ref[rows, cols] = dot_tn(grad_scores, query)
            dv_ref[rows, cols] = dot_tn(weighted, grad)
            if c == 1:
                spot = heads + h
                weight = weight_ref[rows, spot : spot + 1]
                far = dot_nt(grad, first_ref[cols, :])
                gw_ref[rows, spot : spot + 1] = jnp.sum(query_f * far, axis=1, keepdims=True)
                dq = dq + weight * far
                inner_ref[cols, :] = dot_tn(query, (weight * grad.astype(F32)).astype(BF16))
            for level in range(levels):
                spot = (level + 2) * heads + h
                if level < ROW_BITS:
                    state = low_ref[level, cols, :]
                else:
                    state = get_slices(state_ref, h, height, level - ROW_BITS)
                far = dot_nt(grad, state)
                gw_ref[rows, spot : spot + 1] = jnp.sum(query_f * far, axis=1, keepdims=True)
                dq = dq + weight_ref[rows, spot : spot + 1] * far
            dq_ref[rows, cols] = dq.astype(BF16)
    grads = gw_ref[...].T
    blocks = []
    for level in range(all_levels):
        by_row = lax.dot_general(
            grads, onehot_of(index_ref, level), (((1,), (1,)), ((), ())), precision=HIGHEST, preferred_element_type=F32
        )
        blocks.append(by_row[level * heads : (level + 1) * heads])
    joined = [jnp.concatenate(blocks[2 * pair : 2 * pair + 2], axis=1) for pair in range(all_levels // 2)]
    for h in range(0, heads if all_levels % 2 else 0, 2):
        joined.append(jnp.concatenate([blocks[-1][h : h + 1], blocks[-1][h + 1 : h + 2]], axis=1))
    table_ref[...] = jnp.concatenate(joined, axis=0).astype(BF16)


def final_kernel(
    cross_ref, low_ref, inner_ref, key_ref, value_ref, dk_ref, dv_ref, grad_key_ref, grad_value_ref, table_ref, gain_ref
):
    heads = key_ref.shape[1] // CH
    spans = key_ref.shape[0] // CH
    shards = cross_ref.shape[0]
    height = height_of(heads, cross_ref)
    rows = gain_ref.shape[0] // shards
    table_end = cross_ref.shape[1] - height - rows
    total = None
    for s in range(shards):
        tail = cross_ref[s, height:, :].astype(F32)
        total = tail if total is None else total + tail
        gain_ref[s * rows : (s + 1) * rows, :] = tail[table_end:]
    all_levels = table_ref.shape[0]
    for level in range(all_levels):
        if level == all_levels - 1 and all_levels % 2:
            base = (level // 2) * heads
            for h in range(heads):
                spot, left = base + h // 2, (h % 2) * TABLE
                table_ref[level, h : h + 1, :] = total[spot : spot + 1, left : left + TABLE]
        else:
            top, left = (level // 2) * heads, (level % 2) * TABLE
            table_ref[level] = total[top : top + heads, left : left + TABLE]
    for h in range(heads):
        cols = span_rows(h)
        cross = get_slices(cross_ref, h, height).astype(F32) + low_ref[cols, :]
        for c in range(spans):
            rows = span_rows(c)
            state = (cross if c == 1 else inner_ref[cols, :] + cross).astype(BF16)
            grad_key = dk_ref[rows, cols] + dot_nt(value_ref[rows, cols], state)
            grad_value = dv_ref[rows, cols] + dot_nn(key_ref[rows, cols], state)
            grad_key_ref[rows, cols] = grad_key.astype(BF16)
            grad_value_ref[rows, cols] = grad_value.astype(BF16)


def exchange(value, axis):
    return lax.all_to_all(value, axis, split_axis=0, concat_axis=0, tiled=True)


def row_swap(value, mask):
    pairs = [(s, s ^ mask) for s in range(lax.axis_size("seq"))]
    return lax.ppermute(value, "seq", pairs)


def body(queries, key_rows, value_rows, level_table, level_index, norm_gain, cotangent):
    tokens, width = queries.shape
    heads = level_table.shape[2]
    all_levels = level_table.shape[1]
    shards = lax.axis_size("seq")
    columns = lax.axis_size("head")
    levels = shards.bit_length() - 1 - ROW_BITS
    height = heads * CH // shards
    own = tokens // columns
    table_rows = all_levels * heads * TABLE // CH
    gain_rows = columns * heads // shards

    spot = lax.axis_index("seq").reshape(1)

    total, first = span_states(key_rows, value_rows, shards)
    slices = exchange(total, "seq")
    flat = total.reshape(width, CH)
    swaps = [row_swap(flat, mask) for mask in (1, 2, 3)]
    low = call(low_state_kernel, shaped((ROW_BITS, width, CH), BF16), spot, *swaps)
    gain = norm_gain.reshape(1, columns * width)
    table = jnp.transpose(level_table, (1, 2, 0))
    index = jnp.transpose(level_index)
    weights = call(weight_kernel, shaped((tokens, CH), F32), index, table)
    near = call(near_kernel, shaped((tokens, width), F32), queries, key_rows, value_rows, first, low, weights)
    group_states = call(prefix_kernel, shaped((shards, levels * height, CH), BF16), slices)
    states = exchange(group_states, "seq")
    attn = call(far_kernel, shaped((tokens, width), BF16), near, queries, states, weights)
    token_attn = exchange(attn.reshape(columns, own, width), "head")
    normed, token_grad = call(
        norm_kernel,
        (shaped((own, columns * width), BF16), shaped((columns, own + columns, width), BF16)),
        token_attn,
        cotangent,
        gain,
    )
    head_grad = exchange(token_grad, "head")
    grad, groups, low_one, low_two = call(
        grad_kernel,
        (
            pltpu.MemorySpace.HBM((tokens, width), BF16),
            shaped((shards, levels * height + 8, CH), BF16),
            shaped((width, CH), BF16),
            shaped((width, CH), BF16),
        ),
        head_grad,
        queries,
        weights,
        hbm_out=(0,),
        scratch=(pltpu.VMEM((tokens, width), BF16), pltpu.SemaphoreType.DMA),
    )
    group_slices = exchange(groups, "seq")
    swaps = [row_swap(low_one if mask == 1 else low_two, mask) for mask in (1, 2, 3)]
    low_sum = call(low_grad_kernel, shaped((width, CH), F32), spot, *swaps)
    grad_query, near_dk, near_dv, inner, table_part = call(
        back_kernel,
        (
            shaped((tokens, width), BF16),
            shaped((tokens, width), F32),
            shaped((tokens, width), F32),
            shaped((heads * CH, CH), F32),
            shaped((table_rows, CH), BF16),
        ),
        queries,
        key_rows,
        value_rows,
        in_hbm(grad),
        weights,
        states,
        low,
        first,
        index,
        hbm=(3,),
        scratch=(pltpu.VMEM((tokens, CH), F32), pltpu.VMEM((tokens, width), BF16), pltpu.SemaphoreType.DMA),
    )
    key_slices = call(
        suffix_kernel, shaped((shards, height + table_rows + gain_rows, CH), BF16), group_slices, table_part
    )
    cross = exchange(key_slices, "seq")
    grad_key, grad_value, table_sum, gain_sum = call(
        final_kernel,
        (
            shaped((tokens, width), BF16),
            shaped((tokens, width), BF16),
            shaped((all_levels, heads, TABLE), F32),
            shaped((columns * heads, CH), F32),
        ),
        cross,
        low_sum,
        inner,
        key_rows,
        value_rows,
        near_dk,
        near_dv,
    )
    grad_table = jnp.transpose(table_sum, (2, 0, 1))
    return normed, grad_query, grad_key, grad_value, grad_table, gain_sum.reshape(columns * width)


def solution(mesh):
    placed = (
        P("seq", "head"),
        P("seq", "head"),
        P("seq", "head"),
        P(None, None, "head"),
        P("seq", None),
        P(),
        P(("seq", "head"), None),
    )
    return jax.shard_map(
        body,
        mesh=mesh,
        in_specs=placed,
        out_specs=(
            P(("seq", "head"), None),
            P("seq", "head"),
            P("seq", "head"),
            P("seq", "head"),
            P(None, None, "head"),
            P(),
        ),
        check_vma=False,
    )
```

```python
import jax
import jax.numpy as jnp
from jax import lax
from jax.experimental import pallas as pl
from jax.experimental.pallas import tpu as pltpu
from jax.sharding import PartitionSpec as P

CH = 128
TABLE = 64
EPSILON = 1e-06
HIGHEST = lax.Precision.HIGHEST
F32 = jnp.float32
BF16 = jnp.bfloat16
INTERPRET = False
ROW_BITS = 2


def in_hbm(value):
    return pltpu.with_memory_space_constraint(value, pltpu.MemorySpace.HBM)


def call(kernel, out_shape, *operands, hbm=(), hbm_out=(), scratch=()):
    whole = pl.BlockSpec(memory_space=pltpu.VMEM)
    scalar = pl.BlockSpec(memory_space=pltpu.SMEM)
    apart = pl.BlockSpec(memory_space=pltpu.MemorySpace.HBM)
    if isinstance(out_shape, tuple):
        out_specs = tuple(apart if i in hbm_out else whole for i in range(len(out_shape)))
    else:
        out_specs = whole
    return pl.pallas_call(
        kernel,
        out_shape=out_shape,
        in_specs=[
            apart if i in hbm else scalar if operand.ndim == 1 else whole for i, operand in enumerate(operands)
        ],
        out_specs=out_specs,
        scratch_shapes=scratch,
        interpret=INTERPRET,
        compiler_params=pltpu.CompilerParams(vmem_limit_bytes=16 * 1024 * 1024),
    )(*operands)


def shaped(shape, dtype):
    return jax.ShapeDtypeStruct(shape, dtype)


def dot_nn(a, b, precision=None):
    return lax.dot_general(a, b, (((1,), (0,)), ((), ())), precision=precision, preferred_element_type=F32)


def dot_nt(a, b):
    return lax.dot_general(a, b, (((1,), (1,)), ((), ())), preferred_element_type=F32)


def dot_tn(a, b, precision=None):
    return lax.dot_general(a, b, (((0,), (0,)), ((), ())), precision=precision, preferred_element_type=F32)


def causal_mask():
    rows = lax.broadcasted_iota(jnp.int32, (CH, CH), 0)
    cols = lax.broadcasted_iota(jnp.int32, (CH, CH), 1)
    return cols <= rows


def span_rows(c):
    return slice(c * CH, (c + 1) * CH)


def put_slices(ref, value, head, height, level=0):
    per_head = CH // height
    pieces = value.astype(BF16).reshape(per_head, height, value.shape[1])
    ref[head * per_head : (head + 1) * per_head, level * height : (level + 1) * height, :] = pieces


def get_slices(ref, head, height, level=0):
    per_head = CH // height
    pieces = ref[head * per_head : (head + 1) * per_head, level * height : (level + 1) * height, :]
    return pieces.reshape(CH, ref.shape[2])


def height_of(heads, ref):
    return heads * CH // ref.shape[0]


def split_pair(value):
    high = value.astype(BF16)
    return high, (value - high.astype(F32)).astype(BF16)


def state_kernel(key_hbm, value_hbm, total_ref, first_ref, key_ref, value_ref, sems):
    key_copy = pltpu.make_async_copy(key_hbm, key_ref, sems.at[0])
    value_copy = pltpu.make_async_copy(value_hbm, value_ref, sems.at[1])
    key_copy.start()
    value_copy.start()
    key_copy.wait()
    value_copy.wait()
    heads = key_ref.shape[1] // CH
    for h in range(heads):
        cols = span_rows(h)
        first = dot_tn(key_ref[0:CH, cols], value_ref[0:CH, cols])
        second = dot_tn(key_ref[CH : 2 * CH, cols], value_ref[CH : 2 * CH, cols])
        first_ref[cols, :] = first.astype(BF16)
        put_slices(total_ref, first + second, h, total_ref.shape[1])


def span_states(key_rows, value_rows, shards):
    tokens, width = key_rows.shape
    return pl.pallas_call(
        state_kernel,
        out_shape=(shaped((shards, width // shards, CH), BF16), shaped((width, CH), BF16)),
        in_specs=[pl.BlockSpec(memory_space=pltpu.MemorySpace.HBM)] * 2,
        scratch_shapes=[
            pltpu.VMEM((tokens, width), BF16),
            pltpu.VMEM((tokens, width), BF16),
            pltpu.SemaphoreType.DMA((2,)),
        ],
        name="span_states",
        interpret=INTERPRET,
        compiler_params=pltpu.CompilerParams(vmem_limit_bytes=16 * 1024 * 1024),
    )(in_hbm(key_rows), in_hbm(value_rows))


def low_state_kernel(place_ref, one_ref, two_ref, three_ref, state_ref):
    row = place_ref[0] & ((1 << ROW_BITS) - 1)
    one = one_ref[...].astype(F32)
    two = two_ref[...].astype(F32)
    three = three_ref[...].astype(F32)
    state_ref[0] = jnp.where((row & 1) == 1, one, 0.0).astype(BF16)
    pair = jnp.where(row == 2, two + one, jnp.where(row == 3, three + two, 0.0))
    state_ref[1] = pair.astype(BF16)


def low_grad_kernel(one_ref, two_ref, three_ref, sum_ref):
    sum_ref[...] = one_ref[...].astype(F32) + two_ref[...].astype(F32) + three_ref[...].astype(F32)


def prefix_kernel(in_ref, out_ref):
    shards, height = in_ref.shape[0], in_ref.shape[1]
    levels = out_ref.shape[1] // height
    sums = [in_ref[s].astype(F32) for s in range(shards)]
    for _ in range(ROW_BITS):
        sums = [sums[2 * i] + sums[2 * i + 1] for i in range(len(sums) // 2)]
    zero = jnp.zeros(in_ref.shape[1:], BF16)
    for level in range(levels):
        rounded = [s.astype(BF16) for s in sums]
        for t in range(shards):
            group = t >> (level + ROW_BITS)
            out_ref[t, level * height : (level + 1) * height, :] = rounded[group - 1] if group & 1 else zero
        sums = [sums[2 * i] + sums[2 * i + 1] for i in range(len(sums) // 2)]


def suffix_kernel(in_ref, table_ref, out_ref):
    shards = in_ref.shape[0]
    levels = shards.bit_length() - 1 - ROW_BITS
    height = (in_ref.shape[1] - 8) // levels
    start = levels * height
    table_rows = table_ref.shape[0]
    rows = out_ref.shape[1] - height - table_rows
    gain = in_ref[0, start:, :].astype(F32)
    for s in range(1, shards):
        gain = gain + in_ref[s, start:, :].astype(F32)
    gain = (gain[:rows] + gain[rows : 2 * rows]).astype(BF16)
    tail = jnp.concatenate([table_ref[...], gain], axis=0)
    carried = [None]
    for level in range(levels - 1, -1, -1):
        size = 1 << (level + ROW_BITS)
        groups = shards >> (level + ROW_BITS)
        below = []
        for g in range(groups):
            base = carried[g >> 1]
            if g & 1 == 0:
                total = None
                for s in range((g + 1) * size, (g + 2) * size):
                    piece = in_ref[s, level * height : (level + 1) * height, :].astype(F32)
                    total = piece if total is None else total + piece
                base = total if base is None else base + total
            below.append(base)
        carried = below
    zero = jnp.zeros((height, CH), F32)
    for t in range(shards):
        value = zero if carried[t >> ROW_BITS] is None else carried[t >> ROW_BITS]
        out_ref[t, 0:height, :] = value.astype(BF16)
        out_ref[t, height:, :] = tail


def onehot_of(index_ref, level):
    tokens = index_ref.shape[1]
    entry = lax.broadcasted_iota(jnp.int32, (TABLE, tokens), 0)
    return (index_ref[level : level + 1, :] == entry).astype(F32)


def weight_kernel(index_ref, table_ref, weight_ref):
    levels, tokens = index_ref.shape
    heads = table_ref.shape[1]
    rows = [dot_nn(table_ref[level], onehot_of(index_ref, level), HIGHEST) for level in range(levels)]
    rows.append(jnp.zeros((CH - levels * heads, tokens), F32))
    weight_ref[...] = jnp.concatenate(rows, axis=0).T


def near_kernel(query_ref, key_ref, value_ref, first_ref, weight_ref, out_ref):
    heads = query_ref.shape[1] // CH
    spans = query_ref.shape[0] // CH
    causal = causal_mask()
    for c in range(spans):
        rows = span_rows(c)
        for h in range(heads):
            cols = span_rows(h)
            query = query_ref[rows, cols]
            scores = jnp.where(causal, dot_nt(query, key_ref[rows, cols]), 0.0).astype(BF16)
            near = weight_ref[rows, h : h + 1] * dot_nn(scores, value_ref[rows, cols])
            if c == 1:
                near = near + weight_ref[rows, heads + h : heads + h + 1] * dot_nn(query, first_ref[cols, :])
            out_ref[rows, cols] = near


def far_kernel(near_ref, query_ref, state_ref, low_ref, weight_ref, attn_ref):
    heads = query_ref.shape[1] // CH
    spans = query_ref.shape[0] // CH
    height = height_of(heads, state_ref)
    levels = state_ref.shape[1] // height
    for c in range(spans):
        rows = span_rows(c)
        for h in range(heads):
            cols = span_rows(h)
            query = query_ref[rows, cols]
            total = near_ref[rows, cols]
            for level in range(levels + ROW_BITS):
                spot = (level + 2) * heads + h
                if level < ROW_BITS:
                    state = low_ref[level, cols, :]
                else:
                    state = get_slices(state_ref, h, height, level - ROW_BITS)
                total = total + weight_ref[rows, spot : spot + 1] * dot_nn(query, state)
            attn_ref[rows, cols] = total.astype(BF16)


def norm_kernel(attn_ref, cot_ref, gain_ref, normed_ref, grad_ref):
    columns, own, width = attn_ref.shape
    features = float(columns * width)
    squares = jnp.zeros((own, width), F32)
    along = jnp.zeros((own, width), F32)
    for d in range(columns):
        cols = slice(d * width, (d + 1) * width)
        attn = attn_ref[d].astype(F32)
        squares = squares + attn * attn
        along = along + cot_ref[:, cols].astype(F32) * gain_ref[:, cols] * attn
    inv_rms = lax.rsqrt(jnp.sum(squares, axis=1, keepdims=True) / features + EPSILON)
    mean = jnp.sum(along, axis=1, keepdims=True) * inv_rms / features
    parts = []
    for d in range(columns):
        cols = slice(d * width, (d + 1) * width)
        cot = cot_ref[:, cols].astype(F32)
        unit = attn_ref[d].astype(F32) * inv_rms
        normed_ref[:, cols] = (unit * gain_ref[:, cols]).astype(BF16)
        grad_ref[d, 0:own, :] = ((cot * gain_ref[:, cols] - unit * mean) * inv_rms).astype(BF16)
        parts.append(jnp.sum(cot * unit, axis=0, keepdims=True))
    block = jnp.concatenate(parts, axis=0).astype(BF16)
    for d in range(columns):
        grad_ref[d, own:, :] = block


def grad_kernel(place_ref, head_ref, query_ref, weight_ref, grad_hbm, group_ref, one_ref, two_ref, grad_ref, sem):
    columns = head_ref.shape[0]
    own = head_ref.shape[1] - columns
    heads = query_ref.shape[1] // CH
    shards = group_ref.shape[0]
    height = height_of(heads, group_ref)
    levels = group_ref.shape[1] // height
    start = levels * height
    for d in range(columns):
        grad_ref[d * own : (d + 1) * own, :] = head_ref[d, 0:own, :]
    grad_copy = pltpu.make_async_copy(grad_ref, grad_hbm, sem)
    grad_copy.start()
    for h in range(heads):
        cols = span_rows(h)
        grad_f = grad_ref[:, cols].astype(F32)
        query = query_ref[:, cols]
        low = []
        for level in range(levels + ROW_BITS):
            spot = (level + 2) * heads + h
            product = dot_tn(query, (weight_ref[:, spot : spot + 1] * grad_f).astype(BF16))
            if level < ROW_BITS:
                low.append(product)
            else:
                put_slices(group_ref, product, h, height, level - ROW_BITS)
        one_ref[cols, :] = jnp.where((place_ref[0] & 1) == 1, low[0], low[1]).astype(BF16)
        two_ref[cols, :] = low[1].astype(BF16)
    gain = head_ref[0, own:, :].astype(F32)
    for d in range(1, columns):
        gain = gain + head_ref[d, own:, :].astype(F32)
    rows = columns * heads // shards
    extra = group_ref.shape[1] - start
    for s in range(shards):
        spots = range(s * rows, (s + 1) * rows)
        picked = [gain[i // heads : i // heads + 1, span_rows(i % heads)] for i in spots]
        high, low = split_pair(jnp.concatenate(picked, axis=0))
        fill = jnp.zeros((extra - 2 * rows, CH), BF16)
        group_ref[s, start:, :] = jnp.concatenate([high, low, fill], axis=0)
    grad_copy.wait()


def back_kernel(
    query_ref, key_ref, value_ref, grad_hbm, weight_ref, state_ref, low_ref, first_ref, index_ref,
    dq_ref, dk_ref, dv_ref, inner_ref, table_ref, gw_ref, grad_ref, sem,
):
    grad_copy = pltpu.make_async_copy(grad_hbm, grad_ref, sem)
    grad_copy.start()
    grad_copy.wait()
    heads = query_ref.shape[1] // CH
    spans = query_ref.shape[0] // CH
    height = height_of(heads, state_ref)
    levels = state_ref.shape[1] // height + ROW_BITS
    all_levels = levels + 2
    causal = causal_mask()
    gw_ref[...] = jnp.zeros(gw_ref.shape, F32)
    for c in range(spans):
        rows = span_rows(c)
        for h in range(heads):
            cols = span_rows(h)
            query = query_ref[rows, cols]
            query_f = query.astype(F32)
            key = key_ref[rows, cols]
            grad = grad_ref[rows, cols]
            first_weight = weight_ref[rows, h : h + 1]
            scores = jnp.where(causal, dot_nt(query, key), 0.0)
            along = jnp.where(causal, dot_nt(grad, value_ref[rows, cols]), 0.0)
            gw_ref[rows, h : h + 1] = jnp.sum(scores.astype(BF16).astype(F32) * along, axis=1, keepdims=True)
            grad_scores = (along * first_weight).astype(BF16)
            weighted = (scores * first_weight).astype(BF16)
            dq = dot_nn(grad_scores, key)
            dk_ref[rows, cols] = dot_tn(grad_scores, query)
            dv_ref[rows, cols] = dot_tn(weighted, grad)
            if c == 1:
                spot = heads + h
                weight = weight_ref[rows, spot : spot + 1]
                far = dot_nt(grad, first_ref[cols, :])
                gw_ref[rows, spot : spot + 1] = jnp.sum(query_f * far, axis=1, keepdims=True)
                dq = dq + weight * far
                inner_ref[cols, :] = dot_tn(query, (weight * grad.astype(F32)).astype(BF16))
            for level in range(levels):
                spot = (level + 2) * heads + h
                if level < ROW_BITS:
                    state = low_ref[level, cols, :]
                else:
                    state = get_slices(state_ref, h, height, level - ROW_BITS)
                far = dot_nt(grad, state)
                gw_ref[rows, spot : spot + 1] = jnp.sum(query_f * far, axis=1, keepdims=True)
                dq = dq + weight_ref[rows, spot : spot + 1] * far
            dq_ref[rows, cols] = dq.astype(BF16)
    grads = gw_ref[...].T
    blocks = []
    for level in range(all_levels):
        by_row = lax.dot_general(
            grads, onehot_of(index_ref, level), (((1,), (1,)), ((), ())), precision=HIGHEST, preferred_element_type=F32
        )
        blocks.append(by_row[level * heads : (level + 1) * heads])
    joined = [jnp.concatenate(blocks[2 * pair : 2 * pair + 2], axis=1) for pair in range(all_levels // 2)]
    for h in range(0, heads if all_levels % 2 else 0, 2):
        joined.append(jnp.concatenate([blocks[-1][h : h + 1], blocks[-1][h + 1 : h + 2]], axis=1))
    table_ref[...] = jnp.concatenate(joined, axis=0).astype(BF16)


def final_kernel(
    cross_ref, low_ref, inner_ref, key_ref, value_ref, dk_ref, dv_ref, grad_key_ref, grad_value_ref, table_ref, gain_ref
):
    heads = key_ref.shape[1] // CH
    spans = key_ref.shape[0] // CH
    shards = cross_ref.shape[0]
    height = height_of(heads, cross_ref)
    rows = gain_ref.shape[0] // shards
    table_end = cross_ref.shape[1] - height - rows
    total = None
    for s in range(shards):
        tail = cross_ref[s, height:, :].astype(F32)
        total = tail if total is None else total + tail
        gain_ref[s * rows : (s + 1) * rows, :] = tail[table_end:]
    all_levels = table_ref.shape[0]
    for level in range(all_levels):
        if level == all_levels - 1 and all_levels % 2:
            base = (level // 2) * heads
            for h in range(heads):
                spot, left = base + h // 2, (h % 2) * TABLE
                table_ref[level, h : h + 1, :] = total[spot : spot + 1, left : left + TABLE]
        else:
            top, left = (level // 2) * heads, (level % 2) * TABLE
            table_ref[level] = total[top : top + heads, left : left + TABLE]
    for h in range(heads):
        cols = span_rows(h)
        cross = get_slices(cross_ref, h, height).astype(F32) + low_ref[cols, :]
        for c in range(spans):
            rows = span_rows(c)
            state = (cross if c == 1 else inner_ref[cols, :] + cross).astype(BF16)
            grad_key = dk_ref[rows, cols] + dot_nt(value_ref[rows, cols], state)
            grad_value = dv_ref[rows, cols] + dot_nn(key_ref[rows, cols], state)
            grad_key_ref[rows, cols] = grad_key.astype(BF16)
            grad_value_ref[rows, cols] = grad_value.astype(BF16)


def exchange(value, axis):
    return lax.all_to_all(value, axis, split_axis=0, concat_axis=0, tiled=True)


def row_shift(value, step):
    row = 1 << ROW_BITS
    shards = lax.axis_size("seq")
    pairs = [(s, s + step) for s in range(shards) if 0 <= s % row + step < row]
    return lax.ppermute(value, "seq", pairs)


def body(queries, key_rows, value_rows, level_table, level_index, norm_gain, cotangent):
    tokens, width = queries.shape
    heads = level_table.shape[2]
    all_levels = level_table.shape[1]
    shards = lax.axis_size("seq")
    columns = lax.axis_size("head")
    levels = shards.bit_length() - 1 - ROW_BITS
    height = heads * CH // shards
    own = tokens // columns
    table_rows = all_levels * heads * TABLE // CH
    gain_rows = columns * heads // shards

    spot = lax.axis_index("seq").reshape(1)

    total, first = span_states(key_rows, value_rows, shards)
    slices = exchange(total, "seq")
    flat = total.reshape(width, CH)
    shifts = [row_shift(flat, step) for step in (1, 2, 3)]
    low = call(low_state_kernel, shaped((ROW_BITS, width, CH), BF16), spot, *shifts)
    gain = norm_gain.reshape(1, columns * width)
    table = jnp.transpose(level_table, (1, 2, 0))
    index = jnp.transpose(level_index)
    weights = call(weight_kernel, shaped((tokens, CH), F32), index, table)
    near = call(near_kernel, shaped((tokens, width), F32), queries, key_rows, value_rows, first, weights)
    group_states = call(prefix_kernel, shaped((shards, levels * height, CH), BF16), slices)
    states = exchange(group_states, "seq")
    attn = call(far_kernel, shaped((tokens, width), BF16), near, queries, states, low, weights)
    token_attn = exchange(attn.reshape(columns, own, width), "head")
    normed, token_grad = call(
        norm_kernel,
        (shaped((own, columns * width), BF16), shaped((columns, own + columns, width), BF16)),
        token_attn,
        cotangent,
        gain,
    )
    head_grad = exchange(token_grad, "head")
    grad, groups, low_one, low_two = call(
        grad_kernel,
        (
            pltpu.MemorySpace.HBM((tokens, width), BF16),
            shaped((shards, levels * height + 8, CH), BF16),
            shaped((width, CH), BF16),
            shaped((width, CH), BF16),
        ),
        spot,
        head_grad,
        queries,
        weights,
        hbm_out=(0,),
        scratch=(pltpu.VMEM((tokens, width), BF16), pltpu.SemaphoreType.DMA),
    )
    group_slices = exchange(groups, "seq")
    shifts = [row_shift(low_one if step == 1 else low_two, -step) for step in (1, 2, 3)]
    low_sum = call(low_grad_kernel, shaped((width, CH), F32), *shifts)
    grad_query, near_dk, near_dv, inner, table_part = call(
        back_kernel,
        (
            shaped((tokens, width), BF16),
            shaped((tokens, width), F32),
            shaped((tokens, width), F32),
            shaped((heads * CH, CH), F32),
            shaped((table_rows, CH), BF16),
        ),
        queries,
        key_rows,
        value_rows,
        in_hbm(grad),
        weights,
        states,
        low,
        first,
        index,
        hbm=(3,),
        scratch=(pltpu.VMEM((tokens, CH), F32), pltpu.VMEM((tokens, width), BF16), pltpu.SemaphoreType.DMA),
    )
    key_slices = call(
        suffix_kernel, shaped((shards, height + table_rows + gain_rows, CH), BF16), group_slices, table_part
    )
    cross = exchange(key_slices, "seq")
    grad_key, grad_value, table_sum, gain_sum = call(
        final_kernel,
        (
            shaped((tokens, width), BF16),
            shaped((tokens, width), BF16),
            shaped((all_levels, heads, TABLE), F32),
            shaped((columns * heads, CH), F32),
        ),
        cross,
        low_sum,
        inner,
        key_rows,
        value_rows,
        near_dk,
        near_dv,
    )
    grad_table = jnp.transpose(table_sum, (2, 0, 1))
    return normed, grad_query, grad_key, grad_value, grad_table, gain_sum.reshape(columns * width)


def solution(mesh):
    placed = (
        P("seq", "head"),
        P("seq", "head"),
        P("seq", "head"),
        P(None, None, "head"),
        P("seq", None),
        P(),
        P(("seq", "head"), None),
    )
    return jax.shard_map(
        body,
        mesh=mesh,
        in_specs=placed,
        out_specs=(
            P(("seq", "head"), None),
            P("seq", "head"),
            P("seq", "head"),
            P("seq", "head"),
            P(None, None, "head"),
            P(),
        ),
        check_vma=False,
    )
```

```python
import jax
import jax.numpy as jnp
from jax import lax
from jax.experimental import pallas as pl
from jax.experimental.pallas import tpu as pltpu
from jax.sharding import PartitionSpec as P

CH = 128
TABLE = 64
EPSILON = 1e-06
HIGHEST = lax.Precision.HIGHEST
F32 = jnp.float32
BF16 = jnp.bfloat16
INTERPRET = False
ROW_BITS = 2


def in_hbm(value):
    return pltpu.with_memory_space_constraint(value, pltpu.MemorySpace.HBM)


def call(kernel, out_shape, *operands, scratch=()):
    whole = pl.BlockSpec(memory_space=pltpu.VMEM)
    scalar = pl.BlockSpec(memory_space=pltpu.SMEM)
    return pl.pallas_call(
        kernel,
        out_shape=out_shape,
        in_specs=[
            scalar if operand.ndim == 1 else whole for operand in operands
        ],
        scratch_shapes=scratch,
        interpret=INTERPRET,
        compiler_params=pltpu.CompilerParams(vmem_limit_bytes=16 * 1024 * 1024),
    )(*operands)


def shaped(shape, dtype):
    return jax.ShapeDtypeStruct(shape, dtype)


def dot_nn(a, b, precision=None):
    return lax.dot_general(a, b, (((1,), (0,)), ((), ())), precision=precision, preferred_element_type=F32)


def dot_nt(a, b):
    return lax.dot_general(a, b, (((1,), (1,)), ((), ())), preferred_element_type=F32)


def dot_tn(a, b, precision=None):
    return lax.dot_general(a, b, (((0,), (0,)), ((), ())), precision=precision, preferred_element_type=F32)


def causal_mask():
    rows = lax.broadcasted_iota(jnp.int32, (CH, CH), 0)
    cols = lax.broadcasted_iota(jnp.int32, (CH, CH), 1)
    return cols <= rows


def span_rows(c):
    return slice(c * CH, (c + 1) * CH)


def put_slices(ref, value, head, height, level=0):
    per_head = CH // height
    pieces = value.astype(BF16).reshape(per_head, height, value.shape[1])
    ref[head * per_head : (head + 1) * per_head, level * height : (level + 1) * height, :] = pieces


def get_slices(ref, head, height, level=0):
    per_head = CH // height
    pieces = ref[head * per_head : (head + 1) * per_head, level * height : (level + 1) * height, :]
    return pieces.reshape(CH, ref.shape[2])


def height_of(heads, ref):
    return heads * CH // ref.shape[0]


def split_pair(value):
    high = value.astype(BF16)
    return high, (value - high.astype(F32)).astype(BF16)


def state_kernel(key_hbm, value_hbm, total_ref, first_ref, key_ref, value_ref, sems):
    key_copy = pltpu.make_async_copy(key_hbm, key_ref, sems.at[0])
    value_copy = pltpu.make_async_copy(value_hbm, value_ref, sems.at[1])
    key_copy.start()
    value_copy.start()
    key_copy.wait()
    value_copy.wait()
    heads = key_ref.shape[1] // CH
    for h in range(heads):
        cols = span_rows(h)
        first = dot_tn(key_ref[0:CH, cols], value_ref[0:CH, cols])
        second = dot_tn(key_ref[CH : 2 * CH, cols], value_ref[CH : 2 * CH, cols])
        first_ref[cols, :] = first.astype(BF16)
        put_slices(total_ref, first + second, h, total_ref.shape[1])


def span_states(key_rows, value_rows, shards):
    tokens, width = key_rows.shape
    return pl.pallas_call(
        state_kernel,
        out_shape=(shaped((shards, width // shards, CH), BF16), shaped((width, CH), BF16)),
        in_specs=[pl.BlockSpec(memory_space=pltpu.MemorySpace.HBM)] * 2,
        scratch_shapes=[
            pltpu.VMEM((tokens, width), BF16),
            pltpu.VMEM((tokens, width), BF16),
            pltpu.SemaphoreType.DMA((2,)),
        ],
        name="span_states",
        interpret=INTERPRET,
        compiler_params=pltpu.CompilerParams(vmem_limit_bytes=16 * 1024 * 1024),
    )(in_hbm(key_rows), in_hbm(value_rows))


def low_grad_kernel(one_ref, two_ref, three_ref, sum_ref):
    sum_ref[...] = one_ref[...].astype(F32) + two_ref[...].astype(F32) + three_ref[...].astype(F32)


def prefix_kernel(in_ref, out_ref):
    shards, height = in_ref.shape[0], in_ref.shape[1]
    levels = out_ref.shape[1] // height
    sums = [in_ref[s].astype(F32) for s in range(shards)]
    zero = jnp.zeros(in_ref.shape[1:], BF16)
    for level in range(levels):
        rounded = [s.astype(BF16) for s in sums]
        for t in range(shards):
            group = t >> level
            out_ref[t, level * height : (level + 1) * height, :] = rounded[group - 1] if group & 1 else zero
        sums = [sums[2 * i] + sums[2 * i + 1] for i in range(len(sums) // 2)]


def suffix_kernel(in_ref, table_ref, out_ref):
    shards = in_ref.shape[0]
    levels = shards.bit_length() - 1 - ROW_BITS
    height = (in_ref.shape[1] - 8) // levels
    start = levels * height
    table_rows = table_ref.shape[0]
    rows = out_ref.shape[1] - height - table_rows
    gain = in_ref[0, start:, :].astype(F32)
    for s in range(1, shards):
        gain = gain + in_ref[s, start:, :].astype(F32)
    gain = (gain[:rows] + gain[rows : 2 * rows]).astype(BF16)
    tail = jnp.concatenate([table_ref[...], gain], axis=0)
    carried = [None]
    for level in range(levels - 1, -1, -1):
        size = 1 << (level + ROW_BITS)
        groups = shards >> (level + ROW_BITS)
        below = []
        for g in range(groups):
            base = carried[g >> 1]
            if g & 1 == 0:
                total = None
                for s in range((g + 1) * size, (g + 2) * size):
                    piece = in_ref[s, level * height : (level + 1) * height, :].astype(F32)
                    total = piece if total is None else total + piece
                base = total if base is None else base + total
            below.append(base)
        carried = below
    zero = jnp.zeros((height, CH), F32)
    for t in range(shards):
        value = zero if carried[t >> ROW_BITS] is None else carried[t >> ROW_BITS]
        out_ref[t, 0:height, :] = value.astype(BF16)
        out_ref[t, height:, :] = tail


def onehot_of(index_ref, level):
    tokens = index_ref.shape[1]
    entry = lax.broadcasted_iota(jnp.int32, (TABLE, tokens), 0)
    return (index_ref[level : level + 1, :] == entry).astype(F32)


def weight_kernel(index_ref, table_ref, weight_ref):
    levels, tokens = index_ref.shape
    heads = table_ref.shape[1]
    rows = [dot_nn(table_ref[level], onehot_of(index_ref, level), HIGHEST) for level in range(levels)]
    rows.append(jnp.zeros((CH - levels * heads, tokens), F32))
    weight_ref[...] = jnp.concatenate(rows, axis=0).T


def near_kernel(query_ref, key_ref, value_ref, first_ref, weight_ref, out_ref):
    heads = query_ref.shape[1] // CH
    spans = query_ref.shape[0] // CH
    causal = causal_mask()
    for c in range(spans):
        rows = span_rows(c)
        for h in range(heads):
            cols = span_rows(h)
            query = query_ref[rows, cols]
            scores = jnp.where(causal, dot_nt(query, key_ref[rows, cols]), 0.0).astype(BF16)
            near = weight_ref[rows, h : h + 1] * dot_nn(scores, value_ref[rows, cols])
            if c == 1:
                near = near + weight_ref[rows, heads + h : heads + h + 1] * dot_nn(query, first_ref[cols, :])
            out_ref[rows, cols] = near


def far_kernel(near_ref, query_ref, state_ref, weight_ref, attn_ref):
    heads = query_ref.shape[1] // CH
    spans = query_ref.shape[0] // CH
    height = height_of(heads, state_ref)
    levels = state_ref.shape[1] // height
    for c in range(spans):
        rows = span_rows(c)
        for h in range(heads):
            cols = span_rows(h)
            query = query_ref[rows, cols]
            total = near_ref[rows, cols]
            for level in range(levels):
                spot = (level + 2) * heads + h
                state = get_slices(state_ref, h, height, level)
                total = total + weight_ref[rows, spot : spot + 1] * dot_nn(query, state)
            attn_ref[rows, cols] = total.astype(BF16)


def norm_kernel(attn_ref, cot_ref, gain_ref, normed_ref, grad_ref):
    columns, own, width = attn_ref.shape
    features = float(columns * width)
    squares = jnp.zeros((own, width), F32)
    along = jnp.zeros((own, width), F32)
    for d in range(columns):
        cols = slice(d * width, (d + 1) * width)
        attn = attn_ref[d].astype(F32)
        squares = squares + attn * attn
        along = along + cot_ref[:, cols].astype(F32) * gain_ref[:, cols] * attn
    inv_rms = lax.rsqrt(jnp.sum(squares, axis=1, keepdims=True) / features + EPSILON)
    mean = jnp.sum(along, axis=1, keepdims=True) * inv_rms / features
    parts = []
    for d in range(columns):
        cols = slice(d * width, (d + 1) * width)
        cot = cot_ref[:, cols].astype(F32)
        unit = attn_ref[d].astype(F32) * inv_rms
        normed_ref[:, cols] = (unit * gain_ref[:, cols]).astype(BF16)
        grad_ref[d, 0:own, :] = ((cot * gain_ref[:, cols] - unit * mean) * inv_rms).astype(BF16)
        parts.append(jnp.sum(cot * unit, axis=0, keepdims=True))
    block = jnp.concatenate(parts, axis=0).astype(BF16)
    for d in range(columns):
        grad_ref[d, own:, :] = block


def grad_kernel(place_ref, head_ref, query_ref, weight_ref, group_ref, one_ref, two_ref, grad_ref):
    columns = head_ref.shape[0]
    own = head_ref.shape[1] - columns
    heads = query_ref.shape[1] // CH
    shards = group_ref.shape[0]
    height = height_of(heads, group_ref)
    levels = group_ref.shape[1] // height
    start = levels * height
    for d in range(columns):
        grad_ref[d * own : (d + 1) * own, :] = head_ref[d, 0:own, :]
    for h in range(heads):
        cols = span_rows(h)
        grad_f = grad_ref[:, cols].astype(F32)
        query = query_ref[:, cols]
        low = []
        for level in range(levels + ROW_BITS):
            spot = (level + 2) * heads + h
            product = dot_tn(query, (weight_ref[:, spot : spot + 1] * grad_f).astype(BF16))
            if level < ROW_BITS:
                low.append(product)
            else:
                put_slices(group_ref, product, h, height, level - ROW_BITS)
        one_ref[cols, :] = jnp.where((place_ref[0] & 1) == 1, low[0], low[1]).astype(BF16)
        two_ref[cols, :] = low[1].astype(BF16)
    gain = head_ref[0, own:, :].astype(F32)
    for d in range(1, columns):
        gain = gain + head_ref[d, own:, :].astype(F32)
    rows = columns * heads // shards
    extra = group_ref.shape[1] - start
    for s in range(shards):
        spots = range(s * rows, (s + 1) * rows)
        picked = [gain[i // heads : i // heads + 1, span_rows(i % heads)] for i in spots]
        high, low = split_pair(jnp.concatenate(picked, axis=0))
        fill = jnp.zeros((extra - 2 * rows, CH), BF16)
        group_ref[s, start:, :] = jnp.concatenate([high, low, fill], axis=0)


def back_kernel(
    query_ref, key_ref, value_ref, head_ref, weight_ref, state_ref, first_ref, index_ref,
    dq_ref, dk_ref, dv_ref, inner_ref, table_ref, gw_ref, grad_ref,
):
    own = head_ref.shape[1] - head_ref.shape[0]
    for d in range(head_ref.shape[0]):
        grad_ref[d * own : (d + 1) * own, :] = head_ref[d, 0:own, :]
    heads = query_ref.shape[1] // CH
    spans = query_ref.shape[0] // CH
    height = height_of(heads, state_ref)
    levels = state_ref.shape[1] // height
    all_levels = levels + 2
    causal = causal_mask()
    gw_ref[...] = jnp.zeros(gw_ref.shape, F32)
    for c in range(spans):
        rows = span_rows(c)
        for h in range(heads):
            cols = span_rows(h)
            query = query_ref[rows, cols]
            query_f = query.astype(F32)
            key = key_ref[rows, cols]
            grad = grad_ref[rows, cols]
            first_weight = weight_ref[rows, h : h + 1]
            scores = jnp.where(causal, dot_nt(query, key), 0.0)
            along = jnp.where(causal, dot_nt(grad, value_ref[rows, cols]), 0.0)
            gw_ref[rows, h : h + 1] = jnp.sum(scores.astype(BF16).astype(F32) * along, axis=1, keepdims=True)
            grad_scores = (along * first_weight).astype(BF16)
            weighted = (scores * first_weight).astype(BF16)
            dq = dot_nn(grad_scores, key)
            dk_ref[rows, cols] = dot_tn(grad_scores, query)
            dv_ref[rows, cols] = dot_tn(weighted, grad)
            if c == 1:
                spot = heads + h
                weight = weight_ref[rows, spot : spot + 1]
                far = dot_nt(grad, first_ref[cols, :])
                gw_ref[rows, spot : spot + 1] = jnp.sum(query_f * far, axis=1, keepdims=True)
                dq = dq + weight * far
                inner_ref[cols, :] = dot_tn(query, (weight * grad.astype(F32)).astype(BF16))
            for level in range(levels):
                spot = (level + 2) * heads + h
                far = dot_nt(grad, get_slices(state_ref, h, height, level))
                gw_ref[rows, spot : spot + 1] = jnp.sum(query_f * far, axis=1, keepdims=True)
                dq = dq + weight_ref[rows, spot : spot + 1] * far
            dq_ref[rows, cols] = dq.astype(BF16)
    grads = gw_ref[...].T
    blocks = []
    for level in range(all_levels):
        by_row = lax.dot_general(
            grads, onehot_of(index_ref, level), (((1,), (1,)), ((), ())), precision=HIGHEST, preferred_element_type=F32
        )
        blocks.append(by_row[level * heads : (level + 1) * heads])
    joined = [jnp.concatenate(blocks[2 * pair : 2 * pair + 2], axis=1) for pair in range(all_levels // 2)]
    for h in range(0, heads if all_levels % 2 else 0, 2):
        joined.append(jnp.concatenate([blocks[-1][h : h + 1], blocks[-1][h + 1 : h + 2]], axis=1))
    table_ref[...] = jnp.concatenate(joined, axis=0).astype(BF16)


def final_kernel(
    cross_ref, low_ref, inner_ref, key_ref, value_ref, dk_ref, dv_ref, grad_key_ref, grad_value_ref, table_ref, gain_ref
):
    heads = key_ref.shape[1] // CH
    spans = key_ref.shape[0] // CH
    shards = cross_ref.shape[0]
    height = height_of(heads, cross_ref)
    rows = gain_ref.shape[0] // shards
    table_end = cross_ref.shape[1] - height - rows
    total = None
    for s in range(shards):
        tail = cross_ref[s, height:, :].astype(F32)
        total = tail if total is None else total + tail
        gain_ref[s * rows : (s + 1) * rows, :] = tail[table_end:]
    all_levels = table_ref.shape[0]
    for level in range(all_levels):
        if level == all_levels - 1 and all_levels % 2:
            base = (level // 2) * heads
            for h in range(heads):
                spot, left = base + h // 2, (h % 2) * TABLE
                table_ref[level, h : h + 1, :] = total[spot : spot + 1, left : left + TABLE]
        else:
            top, left = (level // 2) * heads, (level % 2) * TABLE
            table_ref[level] = total[top : top + heads, left : left + TABLE]
    for h in range(heads):
        cols = span_rows(h)
        cross = get_slices(cross_ref, h, height).astype(F32) + low_ref[cols, :]
        for c in range(spans):
            rows = span_rows(c)
            state = (cross if c == 1 else inner_ref[cols, :] + cross).astype(BF16)
            grad_key = dk_ref[rows, cols] + dot_nt(value_ref[rows, cols], state)
            grad_value = dv_ref[rows, cols] + dot_nn(key_ref[rows, cols], state)
            grad_key_ref[rows, cols] = grad_key.astype(BF16)
            grad_value_ref[rows, cols] = grad_value.astype(BF16)


def exchange(value, axis):
    return lax.all_to_all(value, axis, split_axis=0, concat_axis=0, tiled=True)


def row_shift(value, step):
    row = 1 << ROW_BITS
    shards = lax.axis_size("seq")
    pairs = [(s, s + step) for s in range(shards) if 0 <= s % row + step < row]
    return lax.ppermute(value, "seq", pairs)


def body(queries, key_rows, value_rows, level_table, level_index, norm_gain, cotangent):
    tokens, width = queries.shape
    heads = level_table.shape[2]
    all_levels = level_table.shape[1]
    shards = lax.axis_size("seq")
    columns = lax.axis_size("head")
    all_bits = shards.bit_length() - 1
    levels = all_bits - ROW_BITS
    height = heads * CH // shards
    own = tokens // columns
    table_rows = all_levels * heads * TABLE // CH
    gain_rows = columns * heads // shards

    spot = lax.axis_index("seq").reshape(1)

    total, first = span_states(key_rows, value_rows, shards)
    slices = exchange(total, "seq")
    gain = norm_gain.reshape(1, columns * width)
    table = jnp.transpose(level_table, (1, 2, 0))
    index = jnp.transpose(level_index)
    weights = call(weight_kernel, shaped((tokens, CH), F32), index, table)
    near = call(near_kernel, shaped((tokens, width), F32), queries, key_rows, value_rows, first, weights)
    group_states = call(prefix_kernel, shaped((shards, all_bits * height, CH), BF16), slices)
    states = exchange(group_states, "seq")
    attn = call(far_kernel, shaped((tokens, width), BF16), near, queries, states, weights)
    token_attn = exchange(attn.reshape(columns, own, width), "head")
    normed, token_grad = call(
        norm_kernel,
        (shaped((own, columns * width), BF16), shaped((columns, own + columns, width), BF16)),
        token_attn,
        cotangent,
        gain,
    )
    head_grad = exchange(token_grad, "head")
    groups, low_one, low_two = call(
        grad_kernel,
        (
            shaped((shards, levels * height + 8, CH), BF16),
            shaped((width, CH), BF16),
            shaped((width, CH), BF16),
        ),
        spot,
        head_grad,
        queries,
        weights,
        scratch=(pltpu.VMEM((tokens, width), BF16),),
    )
    group_slices = exchange(groups, "seq")
    shifts = [row_shift(low_one if step == 1 else low_two, -step) for step in (1, 2, 3)]
    low_sum = call(low_grad_kernel, shaped((width, CH), F32), *shifts)
    grad_query, near_dk, near_dv, inner, table_part = call(
        back_kernel,
        (
            shaped((tokens, width), BF16),
            shaped((tokens, width), F32),
            shaped((tokens, width), F32),
            shaped((heads * CH, CH), F32),
            shaped((table_rows, CH), BF16),
        ),
        queries,
        key_rows,
        value_rows,
        head_grad,
        weights,
        states,
        first,
        index,
        scratch=(pltpu.VMEM((tokens, CH), F32), pltpu.VMEM((tokens, width), BF16)),
    )
    key_slices = call(
        suffix_kernel, shaped((shards, height + table_rows + gain_rows, CH), BF16), group_slices, table_part
    )
    cross = exchange(key_slices, "seq")
    grad_key, grad_value, table_sum, gain_sum = call(
        final_kernel,
        (
            shaped((tokens, width), BF16),
            shaped((tokens, width), BF16),
            shaped((all_levels, heads, TABLE), F32),
            shaped((columns * heads, CH), F32),
        ),
        cross,
        low_sum,
        inner,
        key_rows,
        value_rows,
        near_dk,
        near_dv,
    )
    grad_table = jnp.transpose(table_sum, (2, 0, 1))
    return normed, grad_query, grad_key, grad_value, grad_table, gain_sum.reshape(columns * width)


def solution(mesh):
    placed = (
        P("seq", "head"),
        P("seq", "head"),
        P("seq", "head"),
        P(None, None, "head"),
        P("seq", None),
        P(),
        P(("seq", "head"), None),
    )
    return jax.shard_map(
        body,
        mesh=mesh,
        in_specs=placed,
        out_specs=(
            P(("seq", "head"), None),
            P("seq", "head"),
            P("seq", "head"),
            P("seq", "head"),
            P(None, None, "head"),
            P(),
        ),
        check_vma=False,
    )
```

```python
import jax
import jax.numpy as jnp
from jax import lax
from jax.experimental import pallas as pl
from jax.experimental.pallas import tpu as pltpu
from jax.sharding import PartitionSpec as P

CH = 128
TABLE = 64
EPSILON = 1e-06
HIGHEST = lax.Precision.HIGHEST
F32 = jnp.float32
BF16 = jnp.bfloat16
INTERPRET = False
ROW_BITS = 2


def in_hbm(value):
    return pltpu.with_memory_space_constraint(value, pltpu.MemorySpace.HBM)


def call(kernel, out_shape, *operands, scratch=()):
    whole = pl.BlockSpec(memory_space=pltpu.VMEM)
    scalar = pl.BlockSpec(memory_space=pltpu.SMEM)
    return pl.pallas_call(
        kernel,
        out_shape=out_shape,
        in_specs=[
            scalar if operand.ndim == 1 else whole for operand in operands
        ],
        scratch_shapes=scratch,
        interpret=INTERPRET,
        compiler_params=pltpu.CompilerParams(vmem_limit_bytes=16 * 1024 * 1024),
    )(*operands)


def shaped(shape, dtype):
    return jax.ShapeDtypeStruct(shape, dtype)


def dot_nn(a, b, precision=None):
    return lax.dot_general(a, b, (((1,), (0,)), ((), ())), precision=precision, preferred_element_type=F32)


def dot_nt(a, b):
    return lax.dot_general(a, b, (((1,), (1,)), ((), ())), preferred_element_type=F32)


def dot_tn(a, b, precision=None):
    return lax.dot_general(a, b, (((0,), (0,)), ((), ())), precision=precision, preferred_element_type=F32)


def causal_mask():
    rows = lax.broadcasted_iota(jnp.int32, (CH, CH), 0)
    cols = lax.broadcasted_iota(jnp.int32, (CH, CH), 1)
    return cols <= rows


def span_rows(c):
    return slice(c * CH, (c + 1) * CH)


def put_slices(ref, value, head, height, level=0):
    per_head = CH // height
    pieces = value.astype(BF16).reshape(per_head, height, value.shape[1])
    ref[head * per_head : (head + 1) * per_head, level * height : (level + 1) * height, :] = pieces


def get_slices(ref, head, height, level=0):
    per_head = CH // height
    pieces = ref[head * per_head : (head + 1) * per_head, level * height : (level + 1) * height, :]
    return pieces.reshape(CH, ref.shape[2])


def height_of(heads, ref):
    return heads * CH // ref.shape[0]


def split_pair(value):
    high = value.astype(BF16)
    return high, (value - high.astype(F32)).astype(BF16)


def state_kernel(key_hbm, value_hbm, total_ref, first_ref, key_ref, value_ref, sems):
    key_copy = pltpu.make_async_copy(key_hbm, key_ref, sems.at[0])
    value_copy = pltpu.make_async_copy(value_hbm, value_ref, sems.at[1])
    key_copy.start()
    value_copy.start()
    key_copy.wait()
    value_copy.wait()
    heads = key_ref.shape[1] // CH
    for h in range(heads):
        cols = span_rows(h)
        first = dot_tn(key_ref[0:CH, cols], value_ref[0:CH, cols])
        second = dot_tn(key_ref[CH : 2 * CH, cols], value_ref[CH : 2 * CH, cols])
        first_ref[cols, :] = first.astype(BF16)
        put_slices(total_ref, first + second, h, total_ref.shape[1])


def span_states(key_rows, value_rows, shards):
    tokens, width = key_rows.shape
    return pl.pallas_call(
        state_kernel,
        out_shape=(shaped((shards, width // shards, CH), BF16), shaped((width, CH), BF16)),
        in_specs=[pl.BlockSpec(memory_space=pltpu.MemorySpace.HBM)] * 2,
        scratch_shapes=[
            pltpu.VMEM((tokens, width), BF16),
            pltpu.VMEM((tokens, width), BF16),
            pltpu.SemaphoreType.DMA((2,)),
        ],
        name="span_states",
        interpret=INTERPRET,
        compiler_params=pltpu.CompilerParams(vmem_limit_bytes=16 * 1024 * 1024),
    )(in_hbm(key_rows), in_hbm(value_rows))


def prefix_kernel(in_ref, out_ref):
    shards, height = in_ref.shape[0], in_ref.shape[1]
    levels = out_ref.shape[1] // height
    sums = [in_ref[s].astype(F32) for s in range(shards)]
    zero = jnp.zeros(in_ref.shape[1:], BF16)
    for level in range(levels):
        rounded = [s.astype(BF16) for s in sums]
        for t in range(shards):
            group = t >> level
            out_ref[t, level * height : (level + 1) * height, :] = rounded[group - 1] if group & 1 else zero
        sums = [sums[2 * i] + sums[2 * i + 1] for i in range(len(sums) // 2)]


def suffix_kernel(in_ref, table_ref, out_ref):
    shards = in_ref.shape[0]
    levels = shards.bit_length() - 1 - ROW_BITS
    height = (in_ref.shape[1] - 8) // levels
    start = levels * height
    table_rows = table_ref.shape[0]
    rows = out_ref.shape[1] - height - table_rows
    gain = in_ref[0, start:, :].astype(F32)
    for s in range(1, shards):
        gain = gain + in_ref[s, start:, :].astype(F32)
    gain = (gain[:rows] + gain[rows : 2 * rows]).astype(BF16)
    tail = jnp.concatenate([table_ref[...], gain], axis=0)
    carried = [None]
    for level in range(levels - 1, -1, -1):
        size = 1 << (level + ROW_BITS)
        groups = shards >> (level + ROW_BITS)
        below = []
        for g in range(groups):
            base = carried[g >> 1]
            if g & 1 == 0:
                total = None
                for s in range((g + 1) * size, (g + 2) * size):
                    piece = in_ref[s, level * height : (level + 1) * height, :].astype(F32)
                    total = piece if total is None else total + piece
                base = total if base is None else base + total
            below.append(base)
        carried = below
    zero = jnp.zeros((height, CH), F32)
    for t in range(shards):
        value = zero if carried[t >> ROW_BITS] is None else carried[t >> ROW_BITS]
        out_ref[t, 0:height, :] = value.astype(BF16)
        out_ref[t, height:, :] = tail


def onehot_of(index_ref, level):
    tokens = index_ref.shape[1]
    entry = lax.broadcasted_iota(jnp.int32, (TABLE, tokens), 0)
    return (index_ref[level : level + 1, :] == entry).astype(F32)


def weight_kernel(index_ref, table_ref, weight_ref):
    levels, tokens = index_ref.shape
    heads = table_ref.shape[1]
    rows = [dot_nn(table_ref[level], onehot_of(index_ref, level), HIGHEST) for level in range(levels)]
    rows.append(jnp.zeros((CH - levels * heads, tokens), F32))
    weight_ref[...] = jnp.concatenate(rows, axis=0).T


def near_kernel(query_ref, key_ref, value_ref, first_ref, weight_ref, out_ref):
    heads = query_ref.shape[1] // CH
    spans = query_ref.shape[0] // CH
    causal = causal_mask()
    for c in range(spans):
        rows = span_rows(c)
        for h in range(heads):
            cols = span_rows(h)
            query = query_ref[rows, cols]
            scores = jnp.where(causal, dot_nt(query, key_ref[rows, cols]), 0.0).astype(BF16)
            near = weight_ref[rows, h : h + 1] * dot_nn(scores, value_ref[rows, cols])
            if c == 1:
                near = near + weight_ref[rows, heads + h : heads + h + 1] * dot_nn(query, first_ref[cols, :])
            out_ref[rows, cols] = near


def far_kernel(near_ref, query_ref, state_ref, weight_ref, attn_ref):
    heads = query_ref.shape[1] // CH
    spans = query_ref.shape[0] // CH
    height = height_of(heads, state_ref)
    levels = state_ref.shape[1] // height
    for c in range(spans):
        rows = span_rows(c)
        for h in range(heads):
            cols = span_rows(h)
            query = query_ref[rows, cols]
            total = near_ref[rows, cols]
            for level in range(levels):
                spot = (level + 2) * heads + h
                state = get_slices(state_ref, h, height, level)
                total = total + weight_ref[rows, spot : spot + 1] * dot_nn(query, state)
            attn_ref[rows, cols] = total.astype(BF16)


def norm_kernel(attn_ref, cot_ref, gain_ref, normed_ref, grad_ref):
    columns, own, width = attn_ref.shape
    features = float(columns * width)
    squares = jnp.zeros((own, width), F32)
    along = jnp.zeros((own, width), F32)
    for d in range(columns):
        cols = slice(d * width, (d + 1) * width)
        attn = attn_ref[d].astype(F32)
        squares = squares + attn * attn
        along = along + cot_ref[:, cols].astype(F32) * gain_ref[:, cols] * attn
    inv_rms = lax.rsqrt(jnp.sum(squares, axis=1, keepdims=True) / features + EPSILON)
    mean = jnp.sum(along, axis=1, keepdims=True) * inv_rms / features
    parts = []
    for d in range(columns):
        cols = slice(d * width, (d + 1) * width)
        cot = cot_ref[:, cols].astype(F32)
        unit = attn_ref[d].astype(F32) * inv_rms
        normed_ref[:, cols] = (unit * gain_ref[:, cols]).astype(BF16)
        grad_ref[d, 0:own, :] = ((cot * gain_ref[:, cols] - unit * mean) * inv_rms).astype(BF16)
        parts.append(jnp.sum(cot * unit, axis=0, keepdims=True))
    block = jnp.concatenate(parts, axis=0).astype(BF16)
    for d in range(columns):
        grad_ref[d, own:, :] = block


def grad_kernel(place_ref, head_ref, query_ref, weight_ref, group_ref, one_ref, two_ref, grad_ref):
    columns = head_ref.shape[0]
    own = head_ref.shape[1] - columns
    heads = query_ref.shape[1] // CH
    shards = group_ref.shape[0]
    height = height_of(heads, group_ref)
    levels = group_ref.shape[1] // height
    start = levels * height
    for d in range(columns):
        grad_ref[d * own : (d + 1) * own, :] = head_ref[d, 0:own, :]
    for h in range(heads):
        cols = span_rows(h)
        grad_f = grad_ref[:, cols].astype(F32)
        query = query_ref[:, cols]
        low = []
        for level in range(levels + ROW_BITS):
            spot = (level + 2) * heads + h
            product = dot_tn(query, (weight_ref[:, spot : spot + 1] * grad_f).astype(BF16))
            if level < ROW_BITS:
                low.append(product)
            else:
                put_slices(group_ref, product, h, height, level - ROW_BITS)
        one_ref[cols, :] = jnp.where((place_ref[0] & 1) == 1, low[0], low[1]).astype(BF16)
        two_ref[cols, :] = low[1].astype(BF16)
    gain = head_ref[0, own:, :].astype(F32)
    for d in range(1, columns):
        gain = gain + head_ref[d, own:, :].astype(F32)
    rows = columns * heads // shards
    extra = group_ref.shape[1] - start
    for s in range(shards):
        spots = range(s * rows, (s + 1) * rows)
        picked = [gain[i // heads : i // heads + 1, span_rows(i % heads)] for i in spots]
        high, low = split_pair(jnp.concatenate(picked, axis=0))
        fill = jnp.zeros((extra - 2 * rows, CH), BF16)
        group_ref[s, start:, :] = jnp.concatenate([high, low, fill], axis=0)


def back_kernel(
    query_ref, key_ref, value_ref, head_ref, weight_ref, state_ref, first_ref, index_ref,
    dq_ref, dk_ref, dv_ref, inner_ref, table_ref, gw_ref, grad_ref,
):
    own = head_ref.shape[1] - head_ref.shape[0]
    for d in range(head_ref.shape[0]):
        grad_ref[d * own : (d + 1) * own, :] = head_ref[d, 0:own, :]
    heads = query_ref.shape[1] // CH
    spans = query_ref.shape[0] // CH
    height = height_of(heads, state_ref)
    levels = state_ref.shape[1] // height
    all_levels = levels + 2
    causal = causal_mask()
    gw_ref[...] = jnp.zeros(gw_ref.shape, F32)
    for c in range(spans):
        rows = span_rows(c)
        for h in range(heads):
            cols = span_rows(h)
            query = query_ref[rows, cols]
            query_f = query.astype(F32)
            key = key_ref[rows, cols]
            grad = grad_ref[rows, cols]
            first_weight = weight_ref[rows, h : h + 1]
            scores = jnp.where(causal, dot_nt(query, key), 0.0)
            along = jnp.where(causal, dot_nt(grad, value_ref[rows, cols]), 0.0)
            gw_ref[rows, h : h + 1] = jnp.sum(scores.astype(BF16).astype(F32) * along, axis=1, keepdims=True)
            grad_scores = (along * first_weight).astype(BF16)
            weighted = (scores * first_weight).astype(BF16)
            dq = dot_nn(grad_scores, key)
            dk_ref[rows, cols] = dot_tn(grad_scores, query)
            dv_ref[rows, cols] = dot_tn(weighted, grad)
            if c == 1:
                spot = heads + h
                weight = weight_ref[rows, spot : spot + 1]
                far = dot_nt(grad, first_ref[cols, :])
                gw_ref[rows, spot : spot + 1] = jnp.sum(query_f * far, axis=1, keepdims=True)
                dq = dq + weight * far
                inner_ref[cols, :] = dot_tn(query, (weight * grad.astype(F32)).astype(BF16))
            for level in range(levels):
                spot = (level + 2) * heads + h
                far = dot_nt(grad, get_slices(state_ref, h, height, level))
                gw_ref[rows, spot : spot + 1] = jnp.sum(query_f * far, axis=1, keepdims=True)
                dq = dq + weight_ref[rows, spot : spot + 1] * far
            dq_ref[rows, cols] = dq.astype(BF16)
    grads = gw_ref[...].T
    blocks = []
    for level in range(all_levels):
        by_row = lax.dot_general(
            grads, onehot_of(index_ref, level), (((1,), (1,)), ((), ())), precision=HIGHEST, preferred_element_type=F32
        )
        blocks.append(by_row[level * heads : (level + 1) * heads])
    joined = [jnp.concatenate(blocks[2 * pair : 2 * pair + 2], axis=1) for pair in range(all_levels // 2)]
    for h in range(0, heads if all_levels % 2 else 0, 2):
        joined.append(jnp.concatenate([blocks[-1][h : h + 1], blocks[-1][h + 1 : h + 2]], axis=1))
    table_ref[...] = jnp.concatenate(joined, axis=0).astype(BF16)


def final_kernel(
    cross_ref, one_ref, two_ref, three_ref, inner_ref, key_ref, value_ref, dk_ref, dv_ref, grad_key_ref, grad_value_ref, table_ref, gain_ref
):
    heads = key_ref.shape[1] // CH
    spans = key_ref.shape[0] // CH
    shards = cross_ref.shape[0]
    height = height_of(heads, cross_ref)
    rows = gain_ref.shape[0] // shards
    table_end = cross_ref.shape[1] - height - rows
    total = None
    for s in range(shards):
        tail = cross_ref[s, height:, :].astype(F32)
        total = tail if total is None else total + tail
        gain_ref[s * rows : (s + 1) * rows, :] = tail[table_end:]
    all_levels = table_ref.shape[0]
    for level in range(all_levels):
        if level == all_levels - 1 and all_levels % 2:
            base = (level // 2) * heads
            for h in range(heads):
                spot, left = base + h // 2, (h % 2) * TABLE
                table_ref[level, h : h + 1, :] = total[spot : spot + 1, left : left + TABLE]
        else:
            top, left = (level // 2) * heads, (level % 2) * TABLE
            table_ref[level] = total[top : top + heads, left : left + TABLE]
    for h in range(heads):
        cols = span_rows(h)
        low = one_ref[cols, :].astype(F32) + two_ref[cols, :].astype(F32) + three_ref[cols, :].astype(F32)
        cross = get_slices(cross_ref, h, height).astype(F32) + low
        for c in range(spans):
            rows = span_rows(c)
            state = (cross if c == 1 else inner_ref[cols, :] + cross).astype(BF16)
            grad_key = dk_ref[rows, cols] + dot_nt(value_ref[rows, cols], state)
            grad_value = dv_ref[rows, cols] + dot_nn(key_ref[rows, cols], state)
            grad_key_ref[rows, cols] = grad_key.astype(BF16)
            grad_value_ref[rows, cols] = grad_value.astype(BF16)


def exchange(value, axis):
    return lax.all_to_all(value, axis, split_axis=0, concat_axis=0, tiled=True)


def row_shift(value, step):
    row = 1 << ROW_BITS
    shards = lax.axis_size("seq")
    pairs = [(s, s + step) for s in range(shards) if 0 <= s % row + step < row]
    return lax.ppermute(value, "seq", pairs)


def body(queries, key_rows, value_rows, level_table, level_index, norm_gain, cotangent):
    tokens, width = queries.shape
    heads = level_table.shape[2]
    all_levels = level_table.shape[1]
    shards = lax.axis_size("seq")
    columns = lax.axis_size("head")
    all_bits = shards.bit_length() - 1
    levels = all_bits - ROW_BITS
    height = heads * CH // shards
    own = tokens // columns
    table_rows = all_levels * heads * TABLE // CH
    gain_rows = columns * heads // shards

    spot = lax.axis_index("seq").reshape(1)

    total, first = span_states(key_rows, value_rows, shards)
    slices = exchange(total, "seq")
    gain = norm_gain.reshape(1, columns * width)
    table = jnp.transpose(level_table, (1, 2, 0))
    index = jnp.transpose(level_index)
    weights = call(weight_kernel, shaped((tokens, CH), F32), index, table)
    near = call(near_kernel, shaped((tokens, width), F32), queries, key_rows, value_rows, first, weights)
    group_states = call(prefix_kernel, shaped((shards, all_bits * height, CH), BF16), slices)
    states = exchange(group_states, "seq")
    attn = call(far_kernel, shaped((tokens, width), BF16), near, queries, states, weights)
    token_attn = exchange(attn.reshape(columns, own, width), "head")
    normed, token_grad = call(
        norm_kernel,
        (shaped((own, columns * width), BF16), shaped((columns, own + columns, width), BF16)),
        token_attn,
        cotangent,
        gain,
    )
    head_grad = exchange(token_grad, "head")
    groups, low_one, low_two = call(
        grad_kernel,
        (
            shaped((shards, levels * height + 8, CH), BF16),
            shaped((width, CH), BF16),
            shaped((width, CH), BF16),
        ),
        spot,
        head_grad,
        queries,
        weights,
        scratch=(pltpu.VMEM((tokens, width), BF16),),
    )
    group_slices = exchange(groups, "seq")
    shifts = [row_shift(low_one if step == 1 else low_two, -step) for step in (1, 2, 3)]
    grad_query, near_dk, near_dv, inner, table_part = call(
        back_kernel,
        (
            shaped((tokens, width), BF16),
            shaped((tokens, width), F32),
            shaped((tokens, width), F32),
            shaped((heads * CH, CH), F32),
            shaped((table_rows, CH), BF16),
        ),
        queries,
        key_rows,
        value_rows,
        head_grad,
        weights,
        states,
        first,
        index,
        scratch=(pltpu.VMEM((tokens, CH), F32), pltpu.VMEM((tokens, width), BF16)),
    )
    key_slices = call(
        suffix_kernel, shaped((shards, height + table_rows + gain_rows, CH), BF16), group_slices, table_part
    )
    cross = exchange(key_slices, "seq")
    grad_key, grad_value, table_sum, gain_sum = call(
        final_kernel,
        (
            shaped((tokens, width), BF16),
            shaped((tokens, width), BF16),
            shaped((all_levels, heads, TABLE), F32),
            shaped((columns * heads, CH), F32),
        ),
        cross,
        *shifts,
        inner,
        key_rows,
        value_rows,
        near_dk,
        near_dv,
    )
    grad_table = jnp.transpose(table_sum, (2, 0, 1))
    return normed, grad_query, grad_key, grad_value, grad_table, gain_sum.reshape(columns * width)


def solution(mesh):
    placed = (
        P("seq", "head"),
        P("seq", "head"),
        P("seq", "head"),
        P(None, None, "head"),
        P("seq", None),
        P(),
        P(("seq", "head"), None),
    )
    return jax.shard_map(
        body,
        mesh=mesh,
        in_specs=placed,
        out_specs=(
            P(("seq", "head"), None),
            P("seq", "head"),
            P("seq", "head"),
            P("seq", "head"),
            P(None, None, "head"),
            P(),
        ),
        check_vma=False,
    )
```
